128 devices in a mesh: depth: 8 (over y_lo, x), row: 4 (over y_hi, core), col: 4 (over z).
Axes of the slice: x: 4, y: 4 (y_hi: 2, y_lo: 2; y = y_hi * 2 + y_lo), z: 4, core: 2. Of those that a mesh axis runs over, the one named last changes fastest.
Arguments:
- inputs: bfloat16 [5120, 4096], P(('depth', 'col'), 'row'), may hold values from -6 to 6
- in_bits: int32 [5120, 4096], P(('depth', 'col'), 'row'), may hold values from 0 to 1
- out_grads: bfloat16 [5120, 14336], P(('depth', 'row'), 'col'), may hold values from -6 to 6
- out_bits: int32 [5120, 14336], P(('depth', 'row'), 'col'), may hold values from 0 to 1
- mean_weight: bfloat16 [14336, 4096], P(('col', 'depth'), 'row'), may hold values from -0.09375 to 0.09375
- sigma_weight: bfloat16 [14336, 4096], P(('col', 'depth'), 'row'), may hold values from 0.0049743652 to 0.049804688
- noise: bfloat16 [14336, 4096], P(('col', 'depth'), 'row'), may hold values from -6 to 6
Outputs:
- input_grad: bfloat16 [5120, 4096], P(('depth', 'col'), 'row')
- mean_grad: float32 [14336, 4096], P(('col', 'depth'), 'row')
- sigma_grad: float32 [14336, 4096], P(('col', 'depth'), 'row')
The draws below stay inside these ranges and needn't reach their ends.
All inputs are finite; a program needn't handle non-finite values.
Results may differ from the reference program's by a relative error of at most 0.017.
Values may be sent and summed in bfloat16 or wider, within the bound.
A program may use at most 128 MiB of HBM per device.

```python
import math
import jax
import jax.numpy as jnp
from jax import lax

D = 4096
FF = 14336
SLAB = 640
TOKENS = 5120
N_DEPTH = 8


def set_ends(values, rng, least, largest):
    place = [jax.random.randint(jax.random.fold_in(rng, axis), (), 0, length) for axis, length in enumerate(values.shape)]
    main_axis = values.shape.index(max(values.shape))
    neighbour = place[:main_axis] + [(place[main_axis] + 1) % values.shape[main_axis]] + place[main_axis + 1:]
    return values.at[tuple(place)].set(least).at[tuple(neighbour)].set(largest)


def level_of(key, shape, split, low, high):
    level = 1.0
    for dim, parts in split:
        draws = jax.random.uniform(jax.random.fold_in(jax.random.fold_in(key, 6), dim), (parts,), jnp.float32, low / len(split), high / len(split))
        level = level * jnp.repeat(jnp.exp(draws), shape[dim] // parts).reshape((-1,) + (1,) * (len(shape) - 1 - dim))
    return level


def centred(own_key, shape, spread, limit, cuts=(), kind=jnp.bfloat16):
    level = level_of(own_key, shape, cuts, -0.22, 0.18) if cuts else 1.0
    values = jax.random.normal(own_key, shape, jnp.float32) * spread * level
    return jnp.minimum(jnp.maximum(values, -limit), limit).astype(kind)


def setup_inputs(seed: int = 0) -> dict:
    key_of = jax.random.split(jax.random.key(seed), 8)
    inputs = centred(key_of[0], (TOKENS, D), 1.0, 6.0, ((0, 32), (1, 4)))
    in_bits = set_ends(jax.random.randint(key_of[1], (TOKENS, D), 0, 2), jax.random.fold_in(key_of[1], 1), 0, 1).astype(jnp.int32)
    out_grads = centred(key_of[2], (TOKENS, FF), 1.0, 6.0, ((0, 32), (1, 4)))
    out_bits = set_ends(jax.random.randint(key_of[3], (TOKENS, FF), 0, 2), jax.random.fold_in(key_of[3], 1), 0, 1).astype(jnp.int32)
    mean_weight = centred(key_of[4], (FF, D), D ** -0.5, 0.09375, ((0, 32), (1, 4)))
    sigma_weight = jnp.clip(jnp.exp(math.log(0.049804688) - 2.3038113 * jax.random.uniform(key_of[5], (FF, D), jnp.float32) ** level_of(key_of[5], (FF, D), ((0, 32), (1, 4)), -0.2, 0.2)), 0.0049743652, 0.049804688).astype(jnp.bfloat16)
    noise = centred(key_of[6], (FF, D), 1.0, 6.0, ((0, 32), (1, 4)))
    return dict(inputs=inputs, in_bits=in_bits, out_grads=out_grads, out_bits=out_bits, mean_weight=mean_weight, sigma_weight=sigma_weight, noise=noise)


def reference(inputs, in_bits, out_grads, out_bits, mean_weight, sigma_weight, noise):
    in_sign = (1 - 2 * in_bits).astype(jnp.bfloat16)
    signed_inputs = inputs * in_sign
    signed_grads = out_grads * (1 - 2 * out_bits).astype(jnp.bfloat16)
    perturbed = (sigma_weight.astype(jnp.float32) * noise.astype(jnp.float32)).astype(jnp.bfloat16)
    part_a = jnp.dot(out_grads, mean_weight, preferred_element_type=jnp.float32)
    part_b = jnp.dot(signed_grads, perturbed, preferred_element_type=jnp.float32)
    input_grad = (part_a + part_b * in_sign.astype(jnp.float32)).astype(jnp.bfloat16)

    slab_parts = (inputs.reshape(N_DEPTH, SLAB, D), signed_inputs.reshape(N_DEPTH, SLAB, D),
                  out_grads.reshape(N_DEPTH, SLAB, FF), signed_grads.reshape(N_DEPTH, SLAB, FF))
    dims = (((0,), (0,)), ((), ()))

    def accumulate_slab(running, slab):
        feat_a, feat_b, grad_a, grad_b = slab
        mean_partial = lax.dot_general(grad_a, feat_a, dims, preferred_element_type=jnp.float32).astype(jnp.bfloat16)
        sigma_partial = lax.dot_general(grad_b, feat_b, dims, preferred_element_type=jnp.float32).astype(jnp.bfloat16)
        mean_partial = lax.optimization_barrier(mean_partial)
        sigma_partial = lax.optimization_barrier(sigma_partial)
        return (running[0] + mean_partial.astype(jnp.float32), running[1] + sigma_partial.astype(jnp.float32)), None

    zero_sum = jnp.zeros((FF, D), jnp.float32)
    sums, unused = lax.scan(accumulate_slab, (zero_sum, zero_sum), slab_parts)
    grad_scale = TOKENS ** -0.5
    mean_grad = sums[0] * grad_scale
    sigma_grad = sums[1] * grad_scale * noise.astype(jnp.float32)
    return input_grad, mean_grad, sigma_grad
```

```python
import functools
import jax
import jax.numpy as jnp
from jax import lax
from jax.experimental import pallas as pl
from jax.experimental.pallas import tpu as pltpu
from jax.sharding import PartitionSpec as P

F32 = jnp.float32
BF16 = jnp.bfloat16
MESH = pl.DeviceIdType.MESH


def kernel(scale, w, p, x, s, g, sg, ig, mg, vg,
           wf, pf, gf, sgf, gt, sgt, xf, sf, sxf,
           snd2, sndp, sndm, rhp, rhm, rom, rop, dxs, rz, ysnd, yrcv,
           lsem, xs, xr, zs, zr, ys, yr, cs, cr, ps, pr, ds, dr, es, er):
    depth = lax.axis_index("depth")
    row = lax.axis_index("row")
    z = lax.axis_index("col")
    px = lax.rem(depth, 4)
    ylo = depth // 4
    core = lax.rem(row, 2)
    yhi = row // 2
    y = yhi * 2 + ylo
    olo = 1 - ylo

    def dev(dx=0, dy=0, dz=0, dc=0):
        x2 = lax.rem(px + dx + 4, 4)
        y2 = lax.rem(y + dy + 4, 4)
        return (lax.rem(y2, 2) * 4 + x2, (y2 // 2) * 2 + lax.rem(core + dc, 2), lax.rem(z + dz + 4, 4))

    xp, xm = dev(1), dev(-1)
    zp, zm, z2 = dev(0, 0, 1), dev(0, 0, -1), dev(0, 0, 2)
    yp, ym, y2 = dev(0, 1), dev(0, -1), dev(0, 2)
    pal = dev(0, 0, 0, 1)
    twin = (olo * 4 + px, row, z)

    bar = pltpu.get_barrier_semaphore()
    for other in (xp, xm, zp, zm, z2, yp, ym, y2, pal):
        pl.semaphore_signal(bar, inc=1, device_id=other, device_id_type=MESH)

    local = []

    def here(src, dst, k):
        cp = pltpu.make_async_copy(src, dst, lsem.at[k])
        cp.start()
        local.append(cp)

    sent = []

    def send(src, dst, ssem, rsem, to):
        cp = pltpu.make_async_remote_copy(src_ref=src, dst_ref=dst, send_sem=ssem, recv_sem=rsem,
                                          device_id=to, device_id_type=MESH)
        cp.start()
        sent.append(cp)

    def arrived(dst, rsem):
        pltpu.make_async_remote_copy(src_ref=dst, dst_ref=dst, send_sem=rsem, recv_sem=rsem,
                                     device_id=pal, device_id_type=MESH).wait_recv()

    def wrow(k, h):
        return pl.ds(pl.multiple_of(k * 448 + h * 224, 32), 224)

    def xrow(lo, k, h):
        return pl.ds(pl.multiple_of((lo * 4 + k) * 160 + h * 80, 16), 80)

    def xblk(lo, k):
        return pl.ds(pl.multiple_of((lo * 4 + k) * 160, 32), 160)

    def half(lo):
        return pl.ds(pl.multiple_of(lo * 1792, 128), 1792)

    def nth(a, k):
        return lax.rem(a + k + 4, 4)

    wsrc, wdst = (w, p), (wf, pf)
    xsrc, xdst = (x, s), (xf, sf)
    gsrc, gdst = (g, sg), (gf, sgf)
    for a in range(2):
        here(wsrc[a], wdst[a].at[pl.ds(pl.multiple_of(px * 448, 32), 448)], a)
        here(xsrc[a], xdst[a].at[xblk(ylo, z)], 2 + a)
        here(gsrc[a].at[:, half(ylo)], gdst[a].at[xblk(ylo, row)], 4 + a)
    pl.semaphore_wait(bar, 9)

    for a in range(2):
        send(xsrc[a], xdst[a].at[xblk(ylo, z)], ys.at[6 + a], yr.at[6 + a], twin)
    for h in range(2):
        for a in range(2):
            send(wsrc[a].at[pl.ds(h * 224, 224)], wdst[a].at[wrow(px, h)], xs.at[a, 0, h], xr.at[a, 0, h], xp)
            send(wsrc[a].at[pl.ds((1 - h) * 224, 224)], wdst[a].at[wrow(px, 1 - h)], xs.at[a, 1, h], xr.at[a, 1, h], xm)
    for h in range(2):
        for a in range(2):
            send(xsrc[a].at[pl.ds(h * 80, 80)], xdst[a].at[xrow(ylo, z, h)], zs.at[0, a, 0, h], zr.at[0, a, 0, h], zp)
            send(xsrc[a].at[pl.ds((1 - h) * 80, 80)], xdst[a].at[xrow(ylo, z, 1 - h)],
                 zs.at[0, a, 1, h], zr.at[0, a, 1, h], zm)
    for a in range(2):
        send(gsrc[a].at[:, half(ylo)], gdst[a].at[xblk(ylo, row)], ys.at[4 + a], yr.at[4 + a], y2)
        send(gsrc[a].at[:, half(olo)], gdst[a].at[xblk(ylo, row)], ys.at[a], yr.at[a], yp)
        send(gsrc[a].at[:, half(olo)], gdst[a].at[xblk(ylo, row)], ys.at[2 + a], yr.at[2 + a], ym)
        send(gsrc[a].at[:, half(ylo)], gdst[a].at[xblk(ylo, row)], cs.at[3, a], cr.at[3, a], pal)

    def zring_forward(part, lo):
        for a in range(2):
            arrived(xdst[a].at[xrow(lo, nth(z, -1), 0)], zr.at[part, a, 0, 0])
            send(xdst[a].at[xrow(lo, nth(z, -1), 0)], xdst[a].at[xrow(lo, nth(z, -1), 0)],
                 zs.at[part, a, 0, 2], zr.at[part, a, 0, 2], zp)
            arrived(xdst[a].at[xrow(lo, nth(z, 1), 1)], zr.at[part, a, 1, 0])
            send(xdst[a].at[xrow(lo, nth(z, 1), 1)], xdst[a].at[xrow(lo, nth(z, 1), 1)],
                 zs.at[part, a, 1, 2], zr.at[part, a, 1, 2], zm)

    def zring_rest(part, lo):
        for a in range(2):
            arrived(xdst[a].at[xrow(lo, nth(z, -1), 1)], zr.at[part, a, 0, 1])
            arrived(xdst[a].at[xrow(lo, nth(z, 1), 0)], zr.at[part, a, 1, 1])
            arrived(xdst[a].at[xrow(lo, nth(z, 2), 0)], zr.at[part, a, 0, 2])
            arrived(xdst[a].at[xrow(lo, nth(z, 2), 1)], zr.at[part, a, 1, 2])

    for a in range(2):
        arrived(xdst[a].at[xblk(olo, z)], yr.at[6 + a])
    for h in range(2):
        for a in range(2):
            send(xdst[a].at[xrow(olo, z, h)], xdst[a].at[xrow(olo, z, h)], zs.at[1, a, 0, h], zr.at[1, a, 0, h], zp)
            send(xdst[a].at[xrow(olo, z, 1 - h)], xdst[a].at[xrow(olo, z, 1 - h)],
                 zs.at[1, a, 1, h], zr.at[1, a, 1, h], zm)
    zring_forward(0, ylo)
    for a in range(2):
        arrived(wdst[a].at[wrow(nth(px, -1), 0)], xr.at[a, 0, 0])
        send(wdst[a].at[wrow(nth(px, -1), 0)], wdst[a].at[wrow(nth(px, -1), 0)], xs.at[a, 0, 2], xr.at[a, 0, 2], xp)
        arrived(wdst[a].at[wrow(nth(px, 1), 1)], xr.at[a, 1, 0])
        send(wdst[a].at[wrow(nth(px, 1), 1)], wdst[a].at[wrow(nth(px, 1), 1)], xs.at[a, 1, 2], xr.at[a, 1, 2], xm)
    zring_forward(1, olo)
    below, above = lax.rem(y + 3, 4), lax.rem(y + 1, 4)
    srcs = ((olo, (below // 2) * 2 + core), (olo, (above // 2) * 2 + core), (ylo, (1 - yhi) * 2 + core))
    for k, (lo, r) in enumerate(srcs):
        for a in range(2):
            arrived(gdst[a].at[xblk(lo, r)], yr.at[2 * k + a])
            send(gdst[a].at[xblk(lo, r)], gdst[a].at[xblk(lo, r)], cs.at[k, a], cr.at[k, a], pal)
    zring_rest(0, ylo)
    zring_rest(1, olo)
    for cp in local:
        cp.wait()

    @pl.loop(0, 8)
    def _(i):
        rows = pl.ds(pl.multiple_of(i * 160, 32), 160)
        sxf[rows, :] = xf[rows, :] * sf[rows, :]

    oc = 1 - core
    others = ((olo, (below // 2) * 2 + oc), (olo, (above // 2) * 2 + oc), (ylo, (1 - yhi) * 2 + oc), (ylo, yhi * 2 + oc))
    for k, (lo, r) in enumerate(others):
        for a in range(2):
            arrived(gdst[a].at[xblk(lo, r)], cr.at[k, a])

    first = (7 * nth(px, 2)) // 2
    flips = (gt, sgt)

    def flip(a, start, count):
        def body(i, carry):
            c = lax.rem(first + start + i, 14)
            lanes = pl.ds(pl.multiple_of(c * 128, 128), 128)
            flips[a][lanes, :] = gdst[a][:, lanes].T
            return carry
        lax.fori_loop(0, count, body, 0)

    feats = (xf, sxf)

    def product(a, o, h, dst, extra=None):
        rows = wrow(o, h)

        def body(n, carry):
            cols = pl.ds(pl.multiple_of(n * 256, 256), 256)
            acc = jnp.dot(flips[a][rows, :], feats[a][:, cols], preferred_element_type=F32)
            if extra is not None:
                acc = acc + extra[:, cols].astype(F32)
            dst[:, cols] = acc.astype(dst.dtype)
            return carry
        lax.fori_loop(0, 4, body, 0)

    top, bot = pl.ds(0, 224), pl.ds(224, 224)
    for a in range(2):
        flip(a, 0, 4)
        product(a, nth(px, 2), 0, snd2.at[a, top])
        send(snd2.at[a, top], rhp.at[a], ps.at[a, 0, 0], pr.at[a, 0, 0], xp)
        product(a, nth(px, 2), 1, snd2.at[a, bot])
        send(snd2.at[a, bot], rhm.at[a], ps.at[a, 1, 0], pr.at[a, 1, 0], xm)
    for a in range(2):
        flip(a, 4, 10)
        product(a, nth(px, 1), 1, sndp.at[a, bot])
        send(sndp.at[a, bot], rom.at[a, bot], ps.at[a, 0, 1], pr.at[a, 0, 1], xp)
        product(a, nth(px, -1), 0, sndm.at[a, top])
        send(sndm.at[a, top], rop.at[a, top], ps.at[a, 1, 1], pr.at[a, 1, 1], xm)

    for a in range(2):
        arrived(wdst[a].at[wrow(nth(px, -1), 1)], xr.at[a, 0, 1])
        arrived(wdst[a].at[wrow(nth(px, 1), 0)], xr.at[a, 1, 1])
        arrived(wdst[a].at[wrow(nth(px, 2), 0)], xr.at[a, 0, 2])
        arrived(wdst[a].at[wrow(nth(px, 2), 1)], xr.at[a, 1, 2])
    zto = ((zp, 1), (zm, -1), (z2, 2))
    for j, lo in enumerate((olo, ylo)):
        rows = pl.ds(pl.multiple_of(lo * 640, 128), 640)

        def body(n, carry, rows=rows):
            cols = pl.ds(pl.multiple_of(n * 256, 256), 256)
            a = jnp.dot(gf[rows, :], wf[:, cols], preferred_element_type=F32)
            b = jnp.dot(sgf[rows, :], pf[:, cols], preferred_element_type=F32)
            dxs[rows, cols] = (a + b * sf[rows, cols].astype(F32)).astype(BF16)
            return carry
        lax.fori_loop(0, 4, body, 0)
        for k, (to, dz) in enumerate(zto):
            send(dxs.at[xblk(lo, nth(z, dz))], rz.at[k, j], ds.at[k, j], dr.at[k, j], to)

    for a in range(2):
        arrived(rhp.at[a], pr.at[a, 0, 0])
        product(a, nth(px, 1), 0, sndp.at[a, top], rhp.at[a])
        send(sndp.at[a, top], rom.at[a, top], ps.at[a, 0, 2], pr.at[a, 0, 2], xp)
        arrived(rhm.at[a], pr.at[a, 1, 0])
        product(a, nth(px, -1), 1, sndm.at[a, bot], rhm.at[a])
        send(sndm.at[a, bot], rop.at[a, bot], ps.at[a, 1, 2], pr.at[a, 1, 2], xm)

    def zsum(j, lo):
        for k in range(3):
            arrived(rz.at[k, j], dr.at[k, j])
        own = dxs[xblk(lo, z), :].astype(F32)
        return own + rz[0, j].astype(F32) + rz[1, j].astype(F32) + rz[2, j].astype(F32)

    ysnd[...] = zsum(0, olo).astype(BF16)
    send(ysnd, yrcv, es.at[0], er.at[0], twin)

    outs = (mg, vg)
    for a in range(2):
        for h, part in enumerate((top, bot)):
            product(a, px, h, outs[a].at[part])

    mine = zsum(1, ylo)
    arrived(yrcv, er.at[0])
    ig[...] = (mine + yrcv[...].astype(F32)).astype(BF16)

    for a in range(2):
        for d, (buf, first_rows) in enumerate(((rom, bot), (rop, top))):
            last_rows = top if first_rows is bot else bot
            arrived(buf.at[a, first_rows], pr.at[a, d, 1])
            arrived(buf.at[a, last_rows], pr.at[a, d, 2])

        def body(i, carry, a=a):
            rows = pl.ds(pl.multiple_of(i * 64, 64), 64)
            total = outs[a][rows, :] + rom[a, rows, :].astype(F32) + rop[a, rows, :].astype(F32)
            outs[a][rows, :] = total * scale
            return carry
        lax.fori_loop(0, 7, body, 0)
    for cp in sent:
        cp.wait_send()


def local(inputs, in_bits, out_grads, out_bits, mean_weight, sigma_weight, noise):
    in_sign = (1 - 2 * in_bits).astype(BF16)
    signed_grads = out_grads * (1 - 2 * out_bits).astype(BF16)
    perturbed = (sigma_weight.astype(F32) * noise.astype(F32)).astype(BF16)
    tokens = inputs.shape[0] * lax.axis_size("depth") * lax.axis_size("col")
    any_ = pl.BlockSpec(memory_space=pl.ANY)
    vm = pl.BlockSpec(memory_space=pltpu.VMEM)
    dma = pltpu.SemaphoreType.DMA
    V = pltpu.VMEM
    input_grad, mean_sum, sigma_sum = pl.pallas_call(
        functools.partial(kernel, tokens ** -0.5),
        out_shape=(jax.ShapeDtypeStruct((160, 1024), BF16), jax.ShapeDtypeStruct((448, 1024), F32),
                   jax.ShapeDtypeStruct((448, 1024), F32)),
        in_specs=[any_] * 6,
        out_specs=(vm, vm, vm),
        scratch_shapes=[
            V((1792, 1024), BF16), V((1792, 1024), BF16),
            V((1280, 1792), BF16), V((1280, 1792), BF16),
            V((1792, 1280), BF16), V((1792, 1280), BF16),
            V((1280, 1024), BF16), V((1280, 1024), BF16), V((1280, 1024), BF16),
            V((2, 448, 1024), BF16), V((2, 448, 1024), BF16), V((2, 448, 1024), BF16),
            V((2, 224, 1024), BF16), V((2, 224, 1024), BF16),
            V((2, 448, 1024), BF16), V((2, 448, 1024), BF16),
            V((1280, 1024), BF16), V((3, 2, 160, 1024), BF16),
            V((160, 1024), BF16), V((160, 1024), BF16),
            dma((6,)),
            dma((2, 2, 3)), dma((2, 2, 3)),
            dma((2, 2, 2, 3)), dma((2, 2, 2, 3)),
            dma((8,)), dma((8,)),
            dma((4, 2)), dma((4, 2)),
            dma((2, 2, 3)), dma((2, 2, 3)),
            dma((3, 2)), dma((3, 2)),
            dma((1,)), dma((1,)),
        ],
        compiler_params=pltpu.CompilerParams(collective_id=0, has_side_effects=True, vmem_limit_bytes=60 << 20),
        name="flipout_backward",
    )(mean_weight, perturbed, inputs, in_sign, out_grads, signed_grads)
    return input_grad, mean_sum, sigma_sum * noise.astype(F32)


def solution(mesh):
    placed = (
        P(("depth", "col"), "row"),
        P(("depth", "col"), "row"),
        P(("depth", "row"), "col"),
        P(("depth", "row"), "col"),
        P(("col", "depth"), "row"),
        P(("col", "depth"), "row"),
        P(("col", "depth"), "row"),
    )
    return jax.shard_map(
        local,
        mesh=mesh,
        in_specs=placed,
        out_specs=(
            P(("depth", "col"), "row"),
            P(("col", "depth"), "row"),
            P(("col", "depth"), "row"),
        ),
        check_vma=False,
    )
```

```python
import functools
import jax
import jax.numpy as jnp
from jax import lax
from jax.experimental import pallas as pl
from jax.experimental.pallas import tpu as pltpu
from jax.sharding import PartitionSpec as P

F32 = jnp.float32
BF16 = jnp.bfloat16
MESH = pl.DeviceIdType.MESH


def kernel(scale, w, sig, noise, x, ib, g, ob, ig, mg, vg,
           wf, pf, gf, sgf, gt, sgt, xf, sf, sxf, gfar, sgfar, ibv, obn, obf, nv,
           snd2, sndp, sndm, rhp, rhm, rom, rop, dxs, rz, ysnd, yrcv, igv, sums,
           lsem, osem, xs, xr, zs, zr, ys, yr, ts, tr, cs, cr, ps, pr, ds, dr, es, er):
    depth = lax.axis_index("depth")
    row = lax.axis_index("row")
    z = lax.axis_index("col")
    px = lax.rem(depth, 4)
    ylo = depth // 4
    core = lax.rem(row, 2)
    yhi = row // 2
    y = yhi * 2 + ylo
    olo = 1 - ylo

    def dev(dx=0, dy=0, dz=0, dc=0):
        x2 = lax.rem(px + dx + 4, 4)
        y2 = lax.rem(y + dy + 4, 4)
        return (lax.rem(y2, 2) * 4 + x2, (y2 // 2) * 2 + lax.rem(core + dc, 2), lax.rem(z + dz + 4, 4))

    xp, xm = dev(1), dev(-1)
    zp, zm, z2 = dev(0, 0, 1), dev(0, 0, -1), dev(0, 0, 2)
    yp, ym, y2 = dev(0, 1), dev(0, -1), dev(0, 2)
    pal = dev(0, 0, 0, 1)
    twin = (olo * 4 + px, row, z)

    bar = pltpu.get_barrier_semaphore()
    for other in (xp, xm, zp, zm, z2, yp, ym, y2, pal):
        pl.semaphore_signal(bar, inc=1, device_id=other, device_id_type=MESH)

    def here(src, dst, sem):
        cp = pltpu.make_async_copy(src, dst, sem)
        cp.start()
        return cp

    sent = []

    def send(src, dst, ssem, rsem, to):
        cp = pltpu.make_async_remote_copy(src_ref=src, dst_ref=dst, send_sem=ssem, recv_sem=rsem,
                                          device_id=to, device_id_type=MESH)
        cp.start()
        sent.append(cp)

    def arrived(dst, rsem):
        pltpu.make_async_remote_copy(src_ref=dst, dst_ref=dst, send_sem=rsem, recv_sem=rsem,
                                     device_id=pal, device_id_type=MESH).wait_recv()

    def wrow(k, h):
        return pl.ds(pl.multiple_of(k * 448 + h * 224, 32), 224)

    def xrow(lo, k, h):
        return pl.ds(pl.multiple_of((lo * 4 + k) * 160 + h * 80, 16), 80)

    def xblk(lo, k):
        return pl.ds(pl.multiple_of((lo * 4 + k) * 160, 32), 160)

    def half(lo):
        return pl.ds(pl.multiple_of(lo * 1792, 128), 1792)

    def quarter(q):
        return pl.ds(pl.multiple_of(q * 896, 128), 896)

    def nth(a, k):
        return lax.rem(a + k + 4, 4)

    def rows32(i):
        return pl.ds(pl.multiple_of(i * 32, 32), 32)

    wdst, xdst, gdst = (wf, pf), (xf, sf), (gf, sgf)
    wown = pl.ds(pl.multiple_of(px * 448, 32), 448)
    xown = xblk(ylo, z)
    gown = xblk(ylo, row)
    sv = snd2.at[0]
    load_w = here(w, wf.at[wown], lsem.at[0])
    load_x = here(x, xf.at[xown], lsem.at[1])
    load_ib = here(ib, ibv, lsem.at[2])
    load_gn = here(g.at[:, half(ylo)], gf.at[gown], lsem.at[3])
    load_gf = here(g.at[:, half(olo)], gfar, lsem.at[4])
    load_on = here(ob.at[:, half(ylo)], obn, lsem.at[5])
    load_of = here(ob.at[:, half(olo)], obf, lsem.at[6])
    load_s = here(sig, sv, lsem.at[7])
    load_n = here(noise, nv, lsem.at[8])

    load_x.wait()
    load_ib.wait()

    @pl.loop(0, 5)
    def _(i):
        sf[pl.ds(pl.multiple_of((ylo * 4 + z) * 160 + i * 32, 32), 32), :] = (1 - 2 * ibv[rows32(i), :]).astype(BF16)

    load_w.wait()
    pl.semaphore_wait(bar, 9)

    def send_weights(a):
        for h in range(2):
            send(wdst[a].at[wrow(px, h)], wdst[a].at[wrow(px, h)], xs.at[a, 0, h], xr.at[a, 0, h], xp)
            send(wdst[a].at[wrow(px, 1 - h)], wdst[a].at[wrow(px, 1 - h)], xs.at[a, 1, h], xr.at[a, 1, h], xm)

    def send_feats(part, lo):
        for h in range(2):
            for a in range(2):
                send(xdst[a].at[xrow(lo, z, h)], xdst[a].at[xrow(lo, z, h)],
                     zs.at[part, a, 0, h], zr.at[part, a, 0, h], zp)
                send(xdst[a].at[xrow(lo, z, 1 - h)], xdst[a].at[xrow(lo, z, 1 - h)],
                     zs.at[part, a, 1, h], zr.at[part, a, 1, h], zm)

    gfars = (gfar, sgfar)
    early = 1 - px // 2

    def send_grads(j, a):
        cols = quarter(early if j == 0 else 1 - early)
        near, far = gdst[a].at[gown, cols], gfars[a].at[:, cols]
        send(far, near, ys.at[j, a, 0], yr.at[j, a, 0], yp)
        send(far, near, ys.at[j, a, 1], yr.at[j, a, 1], ym)
        send(near, near, ys.at[j, a, 2], yr.at[j, a, 2], y2)
        send(near, near, cs.at[j, a, 3], cr.at[j, a, 3], pal)

    send_weights(0)
    for a in range(2):
        send(xdst[a].at[xown], xdst[a].at[xown], ts.at[a], tr.at[a], twin)
    send_feats(0, ylo)
    load_gn.wait()
    load_gf.wait()
    send_grads(0, 0)
    load_on.wait()
    load_of.wait()

    @pl.loop(0, 5)
    def _(i):
        rows = rows32(i)
        own = pl.ds(pl.multiple_of((ylo * 4 + row) * 160 + i * 32, 32), 32)
        sgf[own, :] = gf[own, :] * (1 - 2 * obn[rows, :]).astype(BF16)
        sgfar[rows, :] = gfar[rows, :] * (1 - 2 * obf[rows, :]).astype(BF16)

    send_grads(0, 1)
    load_s.wait()
    load_n.wait()

    @pl.loop(0, 14)
    def _(i):
        rows = rows32(i)
        own = pl.ds(pl.multiple_of(px * 448 + i * 32, 32), 32)
        pf[own, :] = (sv[rows, :].astype(F32) * nv[rows, :].astype(F32)).astype(BF16)

    send_weights(1)
    send_grads(1, 0)
    send_grads(1, 1)

    def forward_feats(part, lo):
        for a in range(2):
            lower, upper = xdst[a].at[xrow(lo, nth(z, -1), 0)], xdst[a].at[xrow(lo, nth(z, 1), 1)]
            arrived(lower, zr.at[part, a, 0, 0])
            send(lower, lower, zs.at[part, a, 0, 2], zr.at[part, a, 0, 2], zp)
            arrived(upper, zr.at[part, a, 1, 0])
            send(upper, upper, zs.at[part, a, 1, 2], zr.at[part, a, 1, 2], zm)

    def rest_feats(part, lo):
        for a in range(2):
            arrived(xdst[a].at[xrow(lo, nth(z, -1), 1)], zr.at[part, a, 0, 1])
            arrived(xdst[a].at[xrow(lo, nth(z, 1), 0)], zr.at[part, a, 1, 1])
            arrived(xdst[a].at[xrow(lo, nth(z, 2), 0)], zr.at[part, a, 0, 2])
            arrived(xdst[a].at[xrow(lo, nth(z, 2), 1)], zr.at[part, a, 1, 2])

    def forward_weights(a):
        lower, upper = wdst[a].at[wrow(nth(px, -1), 0)], wdst[a].at[wrow(nth(px, 1), 1)]
        arrived(lower, xr.at[a, 0, 0])
        send(lower, lower, xs.at[a, 0, 2], xr.at[a, 0, 2], xp)
        arrived(upper, xr.at[a, 1, 0])
        send(upper, upper, xs.at[a, 1, 2], xr.at[a, 1, 2], xm)

    def rest_weights(a):
        arrived(wdst[a].at[wrow(nth(px, -1), 1)], xr.at[a, 0, 1])
        arrived(wdst[a].at[wrow(nth(px, 1), 0)], xr.at[a, 1, 1])
        arrived(wdst[a].at[wrow(nth(px, 2), 0)], xr.at[a, 0, 2])
        arrived(wdst[a].at[wrow(nth(px, 2), 1)], xr.at[a, 1, 2])

    below, above = lax.rem(y + 3, 4), lax.rem(y + 1, 4)
    oc = 1 - core

    def forward_grads(j, a):
        cols = quarter(early if j == 0 else 1 - early)
        for k, (lo, hi) in enumerate(((olo, below // 2), (olo, above // 2), (ylo, 1 - yhi))):
            block = gdst[a].at[xblk(lo, hi * 2 + core), cols]
            arrived(block, yr.at[j, a, k])
            send(block, block, cs.at[j, a, k], cr.at[j, a, k], pal)

    def rest_grads(j, a):
        cols = quarter(early if j == 0 else 1 - early)
        for k, (lo, hi) in enumerate(((olo, below // 2), (olo, above // 2), (ylo, 1 - yhi), (ylo, yhi))):
            arrived(gdst[a].at[xblk(lo, hi * 2 + oc), cols], cr.at[j, a, k])

    flips = (gt, sgt)

    def flip(j, a):
        q = early if j == 0 else 1 - early

        def body(i, carry):
            lanes = pl.ds(pl.multiple_of((q * 7 + i) * 128, 128), 128)
            flips[a][lanes, :] = gdst[a][:, lanes].T
            return carry
        lax.fori_loop(0, 7, body, 0)

    feats = (xf, sxf)

    def product(a, rows, dst, extra=None):
        def body(n, carry):
            cols = pl.ds(pl.multiple_of(n * 256, 256), 256)
            acc = jnp.dot(flips[a][rows, :], feats[a][:, cols], preferred_element_type=F32)
            if extra is not None:
                acc = acc + extra[:, cols].astype(F32)
            dst[:, cols] = acc.astype(dst.dtype)
            return carry
        lax.fori_loop(0, 4, body, 0)

    forward_feats(0, ylo)
    forward_weights(0)
    for a in range(2):
        arrived(xdst[a].at[xblk(olo, z)], tr.at[a])
    send_feats(1, olo)
    forward_grads(0, 0)
    forward_feats(1, olo)
    forward_weights(1)
    rest_grads(0, 0)
    flip(0, 0)
    forward_grads(0, 1)
    rest_feats(0, ylo)
    rest_feats(1, olo)

    top, bot = pl.ds(0, 224), pl.ds(224, 224)

    def opposite(a):
        product(a, wrow(nth(px, 2), 0), snd2.at[a, top])
        send(snd2.at[a, top], rhp.at[a], ps.at[a, 0, 0], pr.at[a, 0, 0], xp)
        product(a, wrow(nth(px, 2), 1), snd2.at[a, bot])
        send(snd2.at[a, bot], rhm.at[a], ps.at[a, 1, 0], pr.at[a, 1, 0], xm)

    opposite(0)

    @pl.loop(0, 8)
    def _(i):
        rows = pl.ds(pl.multiple_of(i * 160, 32), 160)
        sxf[rows, :] = xf[rows, :] * sf[rows, :]

    rest_grads(0, 1)
    flip(0, 1)
    opposite(1)
    for a in range(2):
        forward_grads(1, a)
    for a in range(2):
        rest_grads(1, a)
        flip(1, a)
        product(a, wrow(nth(px, 1), 1), sndp.at[a, bot])
        send(sndp.at[a, bot], rom.at[a, bot], ps.at[a, 0, 1], pr.at[a, 0, 1], xp)
        product(a, wrow(nth(px, -1), 0), sndm.at[a, top])
        send(sndm.at[a, top], rop.at[a, top], ps.at[a, 1, 1], pr.at[a, 1, 1], xm)
    rest_weights(0)
    rest_weights(1)

    zto = ((zp, 1), (zm, -1), (z2, 2))

    def input_part(j, lo):
        rows = pl.ds(pl.multiple_of(lo * 640, 128), 640)

        def body(n, carry):
            cols = pl.ds(pl.multiple_of(n * 256, 256), 256)
            a = jnp.dot(gf[rows, :], wf[:, cols], preferred_element_type=F32)
            b = jnp.dot(sgf[rows, :], pf[:, cols], preferred_element_type=F32)
            dxs[rows, cols] = (a + b * sf[rows, cols].astype(F32)).astype(BF16)
            return carry
        lax.fori_loop(0, 4, body, 0)
        for k, (to, dz) in enumerate(zto):
            send(dxs.at[xblk(lo, nth(z, dz))], rz.at[k, j], ds.at[k, j], dr.at[k, j], to)

    def sideways(a):
        arrived(rhp.at[a], pr.at[a, 0, 0])
        product(a, wrow(nth(px, 1), 0), sndp.at[a, top], rhp.at[a])
        send(sndp.at[a, top], rom.at[a, top], ps.at[a, 0, 2], pr.at[a, 0, 2], xp)
        arrived(rhm.at[a], pr.at[a, 1, 0])
        product(a, wrow(nth(px, -1), 1), sndm.at[a, bot], rhm.at[a])
        send(sndm.at[a, bot], rop.at[a, bot], ps.at[a, 1, 2], pr.at[a, 1, 2], xm)

    input_part(0, olo)
    sideways(0)
    input_part(1, ylo)
    sideways(1)

    def zsum(j, lo):
        for k in range(3):
            arrived(rz.at[k, j], dr.at[k, j])
        own = dxs[xblk(lo, z), :].astype(F32)
        return own + rz[0, j].astype(F32) + rz[1, j].astype(F32) + rz[2, j].astype(F32)

    product(0, wown, sums.at[0])
    ysnd[...] = zsum(0, olo).astype(BF16)
    send(ysnd, yrcv, es.at[0], er.at[0], twin)
    product(1, wown, sums.at[1])

    mine = zsum(1, ylo)
    arrived(yrcv, er.at[0])
    igv[...] = (mine + yrcv[...].astype(F32)).astype(BF16)
    stores = [here(igv, ig, osem.at[4])]

    outs = (mg, vg)

    def add(a, h, buf, last):
        def body(i, carry):
            rows = pl.ds(pl.multiple_of(h * 224 + i * 32, 32), 32)
            total = sums[a, rows, :] + buf[a, rows, :].astype(F32)
            if last:
                total = total * scale
                if a == 1:
                    total = total * nv[rows, :].astype(F32)
            sums[a, rows, :] = total
            return carry
        lax.fori_loop(0, 7, body, 0)

    for a in range(2):
        arrived(rom.at[a, bot], pr.at[a, 0, 1])
        add(a, 1, rom, False)
        arrived(rop.at[a, top], pr.at[a, 1, 1])
        add(a, 0, rop, False)
    for a in range(2):
        arrived(rom.at[a, top], pr.at[a, 0, 2])
        add(a, 0, rom, True)
        stores.append(here(sums.at[a, top], outs[a].at[top], osem.at[2 * a]))
        arrived(rop.at[a, bot], pr.at[a, 1, 2])
        add(a, 1, rop, True)
        stores.append(here(sums.at[a, bot], outs[a].at[bot], osem.at[2 * a + 1]))
    for cp in sent:
        cp.wait_send()
    for cp in stores:
        cp.wait()


def local(inputs, in_bits, out_grads, out_bits, mean_weight, sigma_weight, noise):
    tokens = inputs.shape[0] * lax.axis_size("depth") * lax.axis_size("col")
    any_ = pl.BlockSpec(memory_space=pl.ANY)
    dma = pltpu.SemaphoreType.DMA
    V = pltpu.VMEM
    return pl.pallas_call(
        functools.partial(kernel, tokens ** -0.5),
        out_shape=(jax.ShapeDtypeStruct((160, 1024), BF16), jax.ShapeDtypeStruct((448, 1024), F32),
                   jax.ShapeDtypeStruct((448, 1024), F32)),
        in_specs=[any_] * 7,
        out_specs=(any_, any_, any_),
        scratch_shapes=[
            V((1792, 1024), BF16), V((1792, 1024), BF16),
            V((1280, 1792), BF16), V((1280, 1792), BF16),
            V((1792, 1280), BF16), V((1792, 1280), BF16),
            V((1280, 1024), BF16), V((1280, 1024), BF16), V((1280, 1024), BF16),
            V((160, 1792), BF16), V((160, 1792), BF16),
            V((160, 1024), jnp.int32), V((160, 1792), jnp.int32), V((160, 1792), jnp.int32),
            V((448, 1024), BF16),
            V((2, 448, 1024), BF16), V((2, 448, 1024), BF16), V((2, 448, 1024), BF16),
            V((2, 224, 1024), BF16), V((2, 224, 1024), BF16),
            V((2, 448, 1024), BF16), V((2, 448, 1024), BF16),
            V((1280, 1024), BF16), V((3, 2, 160, 1024), BF16),
            V((160, 1024), BF16), V((160, 1024), BF16), V((160, 1024), BF16),
            V((2, 448, 1024), F32),
            dma((9,)), dma((5,)),
            dma((2, 2, 3)), dma((2, 2, 3)),
            dma((2, 2, 2, 3)), dma((2, 2, 2, 3)),
            dma((2, 2, 3)), dma((2, 2, 3)),
            dma((2,)), dma((2,)),
            dma((2, 2, 4)), dma((2, 2, 4)),
            dma((2, 2, 3)), dma((2, 2, 3)),
            dma((3, 2)), dma((3, 2)),
            dma((1,)), dma((1,)),
        ],
        compiler_params=pltpu.CompilerParams(collective_id=0, has_side_effects=True, vmem_limit_bytes=61 << 20),
        name="flipout_backward",
    )(mean_weight, sigma_weight, noise, inputs, in_bits, out_grads, out_bits)


def solution(mesh):
    placed = (
        P(("depth", "col"), "row"),
        P(("depth", "col"), "row"),
        P(("depth", "row"), "col"),
        P(("depth", "row"), "col"),
        P(("col", "depth"), "row"),
        P(("col", "depth"), "row"),
        P(("col", "depth"), "row"),
    )
    return jax.shard_map(
        local,
        mesh=mesh,
        in_specs=placed,
        out_specs=(
            P(("depth", "col"), "row"),
            P(("col", "depth"), "row"),
            P(("col", "depth"), "row"),
        ),
        check_vma=False,
    )
```

```python
import functools
import jax
import jax.numpy as jnp
from jax import lax
from jax.experimental import pallas as pl
from jax.experimental.pallas import tpu as pltpu
from jax.sharding import PartitionSpec as P

F32 = jnp.float32
BF16 = jnp.bfloat16
MESH = pl.DeviceIdType.MESH


def kernel(scale, w, sig, noise, x, ib, g, ob, ig, mg, vg,
           wf, pf, gf, sgf, gt, xf, sf, sxf, gfar, sgfar, ibv, obn, obf, nv,
           snd2, sndp, sndm, rhp, rhm, rom, rop, dxs, rz, ysnd, yrcv,
           lsem, xs, xr, zs, zr, ys, yr, ts, tr, cs, cr, ps, pr, ds, dr, es, er):
    depth = lax.axis_index("depth")
    row = lax.axis_index("row")
    z = lax.axis_index("col")
    px = lax.rem(depth, 4)
    ylo = depth // 4
    core = lax.rem(row, 2)
    yhi = row // 2
    y = yhi * 2 + ylo
    olo = 1 - ylo

    def dev(dx=0, dy=0, dz=0, dc=0):
        x2 = lax.rem(px + dx + 4, 4)
        y2 = lax.rem(y + dy + 4, 4)
        return (lax.rem(y2, 2) * 4 + x2, (y2 // 2) * 2 + lax.rem(core + dc, 2), lax.rem(z + dz + 4, 4))

    xp, xm = dev(1), dev(-1)
    zp, zm, z2 = dev(0, 0, 1), dev(0, 0, -1), dev(0, 0, 2)
    yp, ym, y2 = dev(0, 1), dev(0, -1), dev(0, 2)
    pal = dev(0, 0, 0, 1)
    twin = (olo * 4 + px, row, z)

    bar = pltpu.get_barrier_semaphore()
    for other in (xp, xm, zp, zm, z2, yp, ym, y2, pal):
        pl.semaphore_signal(bar, inc=1, device_id=other, device_id_type=MESH)

    def here(src, dst, sem):
        cp = pltpu.make_async_copy(src, dst, sem)
        cp.start()
        return cp

    sent = []

    def send(src, dst, ssem, rsem, to):
        cp = pltpu.make_async_remote_copy(src_ref=src, dst_ref=dst, send_sem=ssem, recv_sem=rsem,
                                          device_id=to, device_id_type=MESH)
        cp.start()
        sent.append(cp)

    def arrived(dst, rsem):
        pltpu.make_async_remote_copy(src_ref=dst, dst_ref=dst, send_sem=rsem, recv_sem=rsem,
                                     device_id=pal, device_id_type=MESH).wait_recv()

    def wrow(k, h):
        return pl.ds(pl.multiple_of(k * 448 + h * 224, 32), 224)

    def xrow(lo, k, h):
        return pl.ds(pl.multiple_of((lo * 4 + k) * 160 + h * 80, 16), 80)

    def xblk(lo, k):
        return pl.ds(pl.multiple_of((lo * 4 + k) * 160, 32), 160)

    def half(lo):
        return pl.ds(pl.multiple_of(lo * 1792, 128), 1792)

    def quarter(q):
        return pl.ds(pl.multiple_of(q * 896, 128), 896)

    def nth(a, k):
        return lax.rem(a + k + 4, 4)

    def rows32(i):
        return pl.ds(pl.multiple_of(i * 32, 32), 32)

    wdst, xdst, gdst = (wf, pf), (xf, sf), (gf, sgf)
    wown = pl.ds(pl.multiple_of(px * 448, 32), 448)
    xown = xblk(ylo, z)
    gown = xblk(ylo, row)
    sv = snd2.at[0]
    load_w = here(w, wf.at[wown], lsem.at[0])
    load_x = here(x, xf.at[xown], lsem.at[1])
    load_ib = here(ib, ibv, lsem.at[2])
    load_gn = here(g.at[:, half(ylo)], gf.at[gown], lsem.at[3])
    load_gf = here(g.at[:, half(olo)], gfar, lsem.at[4])
    load_on = here(ob.at[:, half(ylo)], obn, lsem.at[5])
    load_of = here(ob.at[:, half(olo)], obf, lsem.at[6])
    load_s = here(sig, sv, lsem.at[7])
    load_n = here(noise, nv, lsem.at[8])

    load_x.wait()
    load_ib.wait()

    @pl.loop(0, 5)
    def _(i):
        sf[pl.ds(pl.multiple_of((ylo * 4 + z) * 160 + i * 32, 32), 32), :] = (1 - 2 * ibv[rows32(i), :]).astype(BF16)

    load_w.wait()
    pl.semaphore_wait(bar, 9)

    def send_weights(a):
        for h in range(2):
            send(wdst[a].at[wrow(px, h)], wdst[a].at[wrow(px, h)], xs.at[a, 0, h], xr.at[a, 0, h], xp)
            send(wdst[a].at[wrow(px, 1 - h)], wdst[a].at[wrow(px, 1 - h)], xs.at[a, 1, h], xr.at[a, 1, h], xm)

    def send_feats(part, lo):
        for h in range(2):
            for a in range(2):
                send(xdst[a].at[xrow(lo, z, h)], xdst[a].at[xrow(lo, z, h)],
                     zs.at[part, a, 0, h], zr.at[part, a, 0, h], zp)
                send(xdst[a].at[xrow(lo, z, 1 - h)], xdst[a].at[xrow(lo, z, 1 - h)],
                     zs.at[part, a, 1, h], zr.at[part, a, 1, h], zm)

    gfars = (gfar, sgfar)
    early = 1 - px // 2

    def send_grads(j, a):
        cols = quarter(early if j == 0 else 1 - early)
        near, far = gdst[a].at[gown, cols], gfars[a].at[:, cols]
        send(far, near, ys.at[j, a, 0], yr.at[j, a, 0], yp)
        send(far, near, ys.at[j, a, 1], yr.at[j, a, 1], ym)
        send(near, near, ys.at[j, a, 2], yr.at[j, a, 2], y2)
        send(near, near, cs.at[j, a, 3], cr.at[j, a, 3], pal)

    send_weights(0)
    for a in range(2):
        send(xdst[a].at[xown], xdst[a].at[xown], ts.at[a], tr.at[a], twin)
    send_feats(0, ylo)
    load_gn.wait()
    load_gf.wait()
    send_grads(0, 0)
    load_on.wait()
    load_of.wait()

    @pl.loop(0, 5)
    def _(i):
        rows = rows32(i)
        own = pl.ds(pl.multiple_of((ylo * 4 + row) * 160 + i * 32, 32), 32)
        sgf[own, :] = gf[own, :] * (1 - 2 * obn[rows, :]).astype(BF16)
        sgfar[rows, :] = gfar[rows, :] * (1 - 2 * obf[rows, :]).astype(BF16)

    send_grads(0, 1)
    load_s.wait()
    load_n.wait()

    @pl.loop(0, 14)
    def _(i):
        rows = rows32(i)
        own = pl.ds(pl.multiple_of(px * 448 + i * 32, 32), 32)
        pf[own, :] = (sv[rows, :].astype(F32) * nv[rows, :].astype(F32)).astype(BF16)

    send_weights(1)
    send_grads(1, 0)
    send_grads(1, 1)

    def forward_feats(part, lo):
        for a in range(2):
            lower, upper = xdst[a].at[xrow(lo, nth(z, -1), 0)], xdst[a].at[xrow(lo, nth(z, 1), 1)]
            arrived(lower, zr.at[part, a, 0, 0])
            send(lower, lower, zs.at[part, a, 0, 2], zr.at[part, a, 0, 2], zp)
            arrived(upper, zr.at[part, a, 1, 0])
            send(upper, upper, zs.at[part, a, 1, 2], zr.at[part, a, 1, 2], zm)

    def rest_feats(part, lo):
        for a in range(2):
            arrived(xdst[a].at[xrow(lo, nth(z, -1), 1)], zr.at[part, a, 0, 1])
            arrived(xdst[a].at[xrow(lo, nth(z, 1), 0)], zr.at[part, a, 1, 1])
            arrived(xdst[a].at[xrow(lo, nth(z, 2), 0)], zr.at[part, a, 0, 2])
            arrived(xdst[a].at[xrow(lo, nth(z, 2), 1)], zr.at[part, a, 1, 2])

    def forward_weights(a):
        lower, upper = wdst[a].at[wrow(nth(px, -1), 0)], wdst[a].at[wrow(nth(px, 1), 1)]
        arrived(lower, xr.at[a, 0, 0])
        send(lower, lower, xs.at[a, 0, 2], xr.at[a, 0, 2], xp)
        arrived(upper, xr.at[a, 1, 0])
        send(upper, upper, xs.at[a, 1, 2], xr.at[a, 1, 2], xm)

    def rest_weights(a):
        arrived(wdst[a].at[wrow(nth(px, -1), 1)], xr.at[a, 0, 1])
        arrived(wdst[a].at[wrow(nth(px, 1), 0)], xr.at[a, 1, 1])
        arrived(wdst[a].at[wrow(nth(px, 2), 0)], xr.at[a, 0, 2])
        arrived(wdst[a].at[wrow(nth(px, 2), 1)], xr.at[a, 1, 2])

    below, above = lax.rem(y + 3, 4), lax.rem(y + 1, 4)
    oc = 1 - core

    def forward_grads(j, a):
        cols = quarter(early if j == 0 else 1 - early)
        for k, (lo, hi) in enumerate(((olo, below // 2), (olo, above // 2), (ylo, 1 - yhi))):
            block = gdst[a].at[xblk(lo, hi * 2 + core), cols]
            arrived(block, yr.at[j, a, k])
            send(block, block, cs.at[j, a, k], cr.at[j, a, k], pal)

    def rest_grads(j, a):
        cols = quarter(early if j == 0 else 1 - early)
        for k, (lo, hi) in enumerate(((olo, below // 2), (olo, above // 2), (ylo, 1 - yhi), (ylo, yhi))):
            arrived(gdst[a].at[xblk(lo, hi * 2 + oc), cols], cr.at[j, a, k])

    feats = (xf, sxf)

    def product(a, start, dst, extra=None):
        chunk = lax.min(start // 128, (start // 896) * 7 + 4)
        for i in range(3):
            lanes = pl.ds(pl.multiple_of((chunk + i) * 128, 128), 128)
            gt[pl.ds(i * 128, 128), :] = gdst[a][:, lanes].T
        rows = pl.ds(pl.multiple_of(start - chunk * 128, 32), 224)

        def body(n, carry):
            cols = pl.ds(pl.multiple_of(n * 256, 256), 256)
            acc = jnp.dot(gt[rows, :], feats[a][:, cols], preferred_element_type=F32)
            if extra is not None:
                acc = acc + extra[:, cols].astype(F32)
            dst[:, cols] = acc.astype(dst.dtype)
            return carry
        lax.fori_loop(0, 4, body, 0)

    def piece(k, h):
        return k * 448 + h * 224

    forward_feats(0, ylo)
    forward_weights(0)
    for a in range(2):
        arrived(xdst[a].at[xblk(olo, z)], tr.at[a])
    send_feats(1, olo)
    forward_grads(0, 0)
    forward_feats(1, olo)
    forward_weights(1)
    rest_grads(0, 0)
    forward_grads(0, 1)
    rest_feats(0, ylo)
    rest_feats(1, olo)

    top, bot = pl.ds(0, 224), pl.ds(224, 224)

    def opposite(a):
        product(a, piece(nth(px, 2), 0), snd2.at[a, top])
        send(snd2.at[a, top], rhp.at[a], ps.at[a, 0, 0], pr.at[a, 0, 0], xp)
        product(a, piece(nth(px, 2), 1), snd2.at[a, bot])
        send(snd2.at[a, bot], rhm.at[a], ps.at[a, 1, 0], pr.at[a, 1, 0], xm)

    opposite(0)

    @pl.loop(0, 8)
    def _(i):
        rows = pl.ds(pl.multiple_of(i * 160, 32), 160)
        sxf[rows, :] = xf[rows, :] * sf[rows, :]

    rest_grads(0, 1)
    opposite(1)
    for a in range(2):
        forward_grads(1, a)
    for a in range(2):
        rest_grads(1, a)
        product(a, piece(nth(px, 1), 1), sndp.at[a, bot])
        send(sndp.at[a, bot], rom.at[a, bot], ps.at[a, 0, 1], pr.at[a, 0, 1], xp)
        product(a, piece(nth(px, -1), 0), sndm.at[a, top])
        send(sndm.at[a, top], rop.at[a, top], ps.at[a, 1, 1], pr.at[a, 1, 1], xm)
    rest_weights(0)
    rest_weights(1)

    zto = ((zp, 1), (zm, -1), (z2, 2))

    def input_part(j, lo):
        rows = pl.ds(pl.multiple_of(lo * 640, 128), 640)

        def body(n, carry):
            cols = pl.ds(pl.multiple_of(n * 256, 256), 256)
            a = jnp.dot(gf[rows, :], wf[:, cols], preferred_element_type=F32)
            b = jnp.dot(sgf[rows, :], pf[:, cols], preferred_element_type=F32)
            dxs[rows, cols] = (a + b * sf[rows, cols].astype(F32)).astype(BF16)
            return carry
        lax.fori_loop(0, 4, body, 0)
        for k, (to, dz) in enumerate(zto):
            send(dxs.at[xblk(lo, nth(z, dz))], rz.at[k, j], ds.at[k, j], dr.at[k, j], to)

    def sideways(a):
        arrived(rhp.at[a], pr.at[a, 0, 0])
        product(a, piece(nth(px, 1), 0), sndp.at[a, top], rhp.at[a])
        send(sndp.at[a, top], rom.at[a, top], ps.at[a, 0, 2], pr.at[a, 0, 2], xp)
        arrived(rhm.at[a], pr.at[a, 1, 0])
        product(a, piece(nth(px, -1), 1), sndm.at[a, bot], rhm.at[a])
        send(sndm.at[a, bot], rop.at[a, bot], ps.at[a, 1, 2], pr.at[a, 1, 2], xm)

    input_part(0, olo)
    sideways(0)
    input_part(1, ylo)
    sideways(1)

    outs = (mg, vg)

    def zsum(j, lo):
        for k in range(3):
            arrived(rz.at[k, j], dr.at[k, j])
        own = dxs[xblk(lo, z), :].astype(F32)
        return own + rz[0, j].astype(F32) + rz[1, j].astype(F32) + rz[2, j].astype(F32)

    for h, part in enumerate((top, bot)):
        product(0, piece(px, h), outs[0].at[part])
    ysnd[...] = zsum(0, olo).astype(BF16)
    send(ysnd, yrcv, es.at[0], er.at[0], twin)
    for h, part in enumerate((top, bot)):
        product(1, piece(px, h), outs[1].at[part])

    mine = zsum(1, ylo)
    arrived(yrcv, er.at[0])
    ig[...] = (mine + yrcv[...].astype(F32)).astype(BF16)

    def add(a, h, buf, last):
        def body(i, carry):
            rows = pl.ds(pl.multiple_of(h * 224 + i * 32, 32), 32)
            total = outs[a][rows, :] + buf[a, rows, :].astype(F32)
            if last:
                total = total * scale
                if a == 1:
                    total = total * nv[rows, :].astype(F32)
            outs[a][rows, :] = total
            return carry
        lax.fori_loop(0, 7, body, 0)

    for a in range(2):
        arrived(rom.at[a, bot], pr.at[a, 0, 1])
        add(a, 1, rom, False)
        arrived(rop.at[a, top], pr.at[a, 1, 1])
        add(a, 0, rop, False)
    for a in range(2):
        arrived(rom.at[a, top], pr.at[a, 0, 2])
        add(a, 0, rom, True)
        arrived(rop.at[a, bot], pr.at[a, 1, 2])
        add(a, 1, rop, True)
    for cp in sent:
        cp.wait_send()


def settle(a, b, c, oa, ob, oc, sem):
    moves = []
    for i, (src, dst) in enumerate(((b, ob), (c, oc), (a, oa))):
        n = src.shape[0] // 2
        for h in range(2):
            part = pl.ds(h * n, n)
            move = pltpu.make_async_copy(src.at[part], dst.at[part], sem.at[i, h])
            move.start()
            moves.append(move)
    for move in moves:
        move.wait()


def local(inputs, in_bits, out_grads, out_bits, mean_weight, sigma_weight, noise):
    tokens = inputs.shape[0] * lax.axis_size("depth") * lax.axis_size("col")
    hbm = pl.BlockSpec(memory_space=pltpu.HBM)
    dma = pltpu.SemaphoreType.DMA
    V = pltpu.VMEM
    shapes = (jax.ShapeDtypeStruct((160, 1024), BF16), jax.ShapeDtypeStruct((448, 1024), F32),
              jax.ShapeDtypeStruct((448, 1024), F32))
    results = pl.pallas_call(
        functools.partial(kernel, tokens ** -0.5),
        out_shape=tuple(pltpu.VMEM(t.shape, t.dtype) for t in shapes),
        in_specs=[hbm] * 7,
        out_specs=(pl.BlockSpec(memory_space=pltpu.VMEM),) * 3,
        scratch_shapes=[
            V((1792, 1024), BF16), V((1792, 1024), BF16),
            V((1280, 1792), BF16), V((1280, 1792), BF16),
            V((384, 1280), BF16),
            V((1280, 1024), BF16), V((1280, 1024), BF16), V((1280, 1024), BF16),
            V((160, 1792), BF16), V((160, 1792), BF16),
            V((160, 1024), jnp.int32), V((160, 1792), jnp.int32), V((160, 1792), jnp.int32),
            V((448, 1024), BF16),
            V((2, 448, 1024), BF16), V((2, 448, 1024), BF16), V((2, 448, 1024), BF16),
            V((2, 224, 1024), BF16), V((2, 224, 1024), BF16),
            V((2, 448, 1024), BF16), V((2, 448, 1024), BF16),
            V((1280, 1024), BF16), V((3, 2, 160, 1024), BF16),
            V((160, 1024), BF16), V((160, 1024), BF16),
            dma((9,)),
            dma((2, 2, 3)), dma((2, 2, 3)),
            dma((2, 2, 2, 3)), dma((2, 2, 2, 3)),
            dma((2, 2, 3)), dma((2, 2, 3)),
            dma((2,)), dma((2,)),
            dma((2, 2, 4)), dma((2, 2, 4)),
            dma((2, 2, 3)), dma((2, 2, 3)),
            dma((3, 2)), dma((3, 2)),
            dma((1,)), dma((1,)),
        ],
        compiler_params=pltpu.CompilerParams(collective_id=0, has_side_effects=True, vmem_limit_bytes=51 << 20),
        name="flipout_backward",
    )(*[pltpu.with_memory_space_constraint(t, pltpu.HBM) for t in (
        mean_weight, sigma_weight, noise, inputs, in_bits, out_grads, out_bits)])
    return pl.pallas_call(
        settle,
        out_shape=shapes,
        in_specs=[pl.BlockSpec(memory_space=pltpu.VMEM)] * 3,
        out_specs=(hbm, hbm, hbm),
        scratch_shapes=[dma((3, 2))],
        compiler_params=pltpu.CompilerParams(vmem_limit_bytes=8 << 20),
        name="settle",
    )(*results)


def solution(mesh):
    placed = (
        P(("depth", "col"), "row"),
        P(("depth", "col"), "row"),
        P(("depth", "row"), "col"),
        P(("depth", "row"), "col"),
        P(("col", "depth"), "row"),
        P(("col", "depth"), "row"),
        P(("col", "depth"), "row"),
    )
    return jax.shard_map(
        local,
        mesh=mesh,
        in_specs=placed,
        out_specs=(
            P(("depth", "col"), "row"),
            P(("col", "depth"), "row"),
            P(("col", "depth"), "row"),
        ),
        check_vma=False,
    )
```

```python
import functools
import jax
import jax.numpy as jnp
from jax import lax
from jax.experimental import pallas as pl
from jax.experimental.pallas import tpu as pltpu
from jax.sharding import PartitionSpec as P

F32 = jnp.float32
BF16 = jnp.bfloat16
MESH = pl.DeviceIdType.MESH


def kernel(scale, w, sig, noise, x, ib, g, ob, ig, mg, vg,
           wf, pf, gf, sgf, gt, xf, sf, sxf, sxp, gfar, sgfar, sgno, sgfo, parfar, ibv, obn, obf, nv,
           snd2, sndp, sndm, rhp, rhm, rom, rop, ssnd, srcv, dxs, dxp, rfp, rfm, rzm, rzp,
           tsnd, trcv, ysnd, yrcv,
           lsem, xs, xr, zs, zr, us, ur, ys, yr, cs, cr, ts, tr, gs, gr, hs, hr, fs, fr,
           ps, pr, qs, qr, ds, dr, ks, kr, es, er):
    depth = lax.axis_index("depth")
    row = lax.axis_index("row")
    z = lax.axis_index("col")
    px = lax.rem(depth, 4)
    ylo = depth // 4
    core = lax.rem(row, 2)
    yhi = row // 2
    y = yhi * 2 + ylo
    olo = 1 - ylo
    mine = lax.rem(px, 2)
    pair = px // 2
    early = 1 - pair

    def dev(dx=0, dy=0, dz=0, dc=0):
        x2 = lax.rem(px + dx + 4, 4)
        y2 = lax.rem(y + dy + 4, 4)
        return (lax.rem(y2, 2) * 4 + x2, (y2 // 2) * 2 + lax.rem(core + dc, 2), lax.rem(z + dz + 4, 4))

    xp, xm = dev(1), dev(-1)
    zp, zm = dev(0, 0, 1), dev(0, 0, -1)
    yp, ym, y2 = dev(0, 1), dev(0, -1), dev(0, 2)
    pal = dev(0, 0, 0, 1)
    twin = (olo * 4 + px, row, z)
    fmate = (ylo * 4 + px + 1 - 2 * mine, row, z)
    tmate = (ylo * 4 + 3 - px, row, z)

    bar = pltpu.get_barrier_semaphore()
    for other in (xp, xm, zp, zm, yp, ym, y2, pal):
        pl.semaphore_signal(bar, inc=1, device_id=other, device_id_type=MESH)

    def here(src, dst, sem):
        cp = pltpu.make_async_copy(src, dst, sem)
        cp.start()
        return cp

    sent = []

    def send(src, dst, ssem, rsem, to):
        cp = pltpu.make_async_remote_copy(src_ref=src, dst_ref=dst, send_sem=ssem, recv_sem=rsem,
                                          device_id=to, device_id_type=MESH)
        cp.start()
        sent.append(cp)

    def arrived(dst, rsem):
        pltpu.make_async_remote_copy(src_ref=dst, dst_ref=dst, send_sem=rsem, recv_sem=rsem,
                                     device_id=pal, device_id_type=MESH).wait_recv()

    def wrow(k, h):
        return pl.ds(pl.multiple_of(k * 448 + h * 224, 32), 224)

    def xrow(lo, k, h):
        return pl.ds(pl.multiple_of((lo * 4 + k) * 160 + h * 80, 16), 80)

    def xblk(lo, k):
        return pl.ds(pl.multiple_of((lo * 4 + k) * 160, 32), 160)

    def half(lo):
        return pl.ds(pl.multiple_of(lo * 1792, 128), 1792)

    def quarter(q):
        return pl.ds(pl.multiple_of(q * 896, 128), 896)

    def nth(a, k):
        return lax.rem(a + k + 4, 4)

    def rows32(i):
        return pl.ds(pl.multiple_of(i * 32, 32), 32)

    xdst = (xf, sf)
    wown = pl.ds(pl.multiple_of(px * 448, 32), 448)
    xown = xblk(ylo, z)
    gown = xblk(ylo, row)
    load_w = here(w, wf.at[wown], lsem.at[0])
    load_x = here(x, xf.at[xown], lsem.at[1])
    load_ib = here(ib, ibv, lsem.at[2])
    load_gn = here(g.at[:, half(ylo)], gf.at[gown], lsem.at[3])
    load_gf = here(g.at[:, half(olo)], gfar, lsem.at[4])
    load_on = here(ob.at[:, half(ylo)], obn, lsem.at[5])
    load_of = here(ob.at[:, half(olo)], obf, lsem.at[6])
    load_s = here(sig, snd2, lsem.at[7])
    load_n = here(noise, nv, lsem.at[8])

    load_x.wait()
    load_ib.wait()

    @pl.loop(0, 5)
    def _(i):
        rows = pl.ds(pl.multiple_of((ylo * 4 + z) * 160 + i * 32, 32), 32)
        sign = (1 - 2 * ibv[rows32(i), :]).astype(BF16)
        sf[rows, :] = sign
        sxf[rows, :] = xf[rows, :] * sign

    load_w.wait()
    pl.semaphore_wait(bar, 8)

    def send_weights(h):
        send(wf.at[wrow(px, h)], wf.at[wrow(px, h)], xs.at[0, h], xr.at[0, h], xp)
        send(wf.at[wrow(px, 1 - h)], wf.at[wrow(px, 1 - h)], xs.at[1, h], xr.at[1, h], xm)

    def send_feats(part, lo):
        for h in range(2):
            for a in range(2):
                send(xdst[a].at[xrow(lo, z, h)], xdst[a].at[xrow(lo, z, h)],
                     zs.at[part, a, 0, h], zr.at[part, a, 0, h], zp)
                send(xdst[a].at[xrow(lo, z, 1 - h)], xdst[a].at[xrow(lo, z, 1 - h)],
                     zs.at[part, a, 1, h], zr.at[part, a, 1, h], zm)

    def place(fam, lo, r):
        if fam < 2:
            return gf.at[xblk(lo, r), quarter(early if fam == 0 else pair)]
        return sgf.at[pl.ds(pl.multiple_of((fam - 2) * 1280 + (lo * 4 + r) * 160, 32), 160)]

    def send_grads(fam):
        near = place(fam, ylo, row)
        if fam < 2:
            far = gfar.at[:, quarter(early if fam == 0 else pair)]
        else:
            far = sgfar if fam == 2 else parfar
        send(far, near, ys.at[fam, 0], yr.at[fam, 0], yp)
        send(far, near, ys.at[fam, 1], yr.at[fam, 1], ym)
        send(near, near, ys.at[fam, 2], yr.at[fam, 2], y2)
        send(near, near, cs.at[fam, 3], cr.at[fam, 3], pal)

    send_weights(0)
    for a in range(2):
        send(xdst[a].at[xown], xdst[a].at[xown], ts.at[a], tr.at[a], twin)
    send_feats(0, ylo)
    load_gn.wait()
    load_gf.wait()
    send_grads(0)
    load_on.wait()
    load_of.wait()

    @pl.loop(0, 5)
    def _(i):
        rows = rows32(i)
        own = pl.ds(pl.multiple_of((ylo * 4 + row) * 160 + i * 32, 32), 32)
        qa, qb = quarter(pair), quarter(early)
        sgf[own, :] = gf[own, qa] * (1 - 2 * obn[rows, qa]).astype(BF16)
        sgfar[rows, :] = gfar[rows, qa] * (1 - 2 * obf[rows, qa]).astype(BF16)
        sgno[rows, :] = gf[own, qb] * (1 - 2 * obn[rows, qb]).astype(BF16)
        sgfo[rows, :] = gfar[rows, qb] * (1 - 2 * obf[rows, qb]).astype(BF16)

    send(sgfo, parfar, gs.at[0], gr.at[0], tmate)
    send(sgno, place(3, ylo, row), gs.at[1], gr.at[1], tmate)
    send(sxf.at[xown], sxp.at[xown], hs.at[0], hr.at[0], tmate)
    load_s.wait()
    load_n.wait()

    @pl.loop(0, 14)
    def _(i):
        rows = rows32(i)
        own = pl.ds(pl.multiple_of(mine * 448 + i * 32, 32), 32)
        pf[own, :] = (snd2[rows, :].astype(F32) * nv[rows, :].astype(F32)).astype(BF16)

    for h in range(2):
        send(pf.at[wrow(mine, h)], pf.at[wrow(mine, h)], fs.at[h], fr.at[h], fmate)
    send_grads(1)

    def forward_feats(part, lo):
        for a in range(2):
            lower, upper = xdst[a].at[xrow(lo, nth(z, -1), 0)], xdst[a].at[xrow(lo, nth(z, 1), 1)]
            arrived(lower, zr.at[part, a, 0, 0])
            send(lower, lower, zs.at[part, a, 0, 2], zr.at[part, a, 0, 2], zp)
            arrived(upper, zr.at[part, a, 1, 0])
            send(upper, upper, zs.at[part, a, 1, 2], zr.at[part, a, 1, 2], zm)

    def rest_feats(part, lo):
        for a in range(2):
            arrived(xdst[a].at[xrow(lo, nth(z, -1), 1)], zr.at[part, a, 0, 1])
            arrived(xdst[a].at[xrow(lo, nth(z, 1), 0)], zr.at[part, a, 1, 1])
            arrived(xdst[a].at[xrow(lo, nth(z, 2), 0)], zr.at[part, a, 0, 2])
            arrived(xdst[a].at[xrow(lo, nth(z, 2), 1)], zr.at[part, a, 1, 2])

    def send_mates(part, lo):
        arrived(sxp.at[xblk(lo, z)], hr.at[part])
        for h in range(2):
            send(sxp.at[xrow(lo, z, h)], sxp.at[xrow(lo, z, h)], us.at[part, 0, h], ur.at[part, 0, h], zp)
            send(sxp.at[xrow(lo, z, 1 - h)], sxp.at[xrow(lo, z, 1 - h)], us.at[part, 1, h], ur.at[part, 1, h], zm)

    def forward_mates(part, lo):
        lower, upper = sxp.at[xrow(lo, nth(z, -1), 0)], sxp.at[xrow(lo, nth(z, 1), 1)]
        arrived(lower, ur.at[part, 0, 0])
        send(lower, lower, us.at[part, 0, 2], ur.at[part, 0, 2], zp)
        arrived(upper, ur.at[part, 1, 0])
        send(upper, upper, us.at[part, 1, 2], ur.at[part, 1, 2], zm)

    def rest_mates(part, lo):
        arrived(sxp.at[xrow(lo, nth(z, -1), 1)], ur.at[part, 0, 1])
        arrived(sxp.at[xrow(lo, nth(z, 1), 0)], ur.at[part, 1, 1])
        arrived(sxp.at[xrow(lo, nth(z, 2), 0)], ur.at[part, 0, 2])
        arrived(sxp.at[xrow(lo, nth(z, 2), 1)], ur.at[part, 1, 2])

    def forward_weights():
        lower, upper = wf.at[wrow(nth(px, -1), 0)], wf.at[wrow(nth(px, 1), 1)]
        arrived(lower, xr.at[0, 0])
        send(lower, lower, xs.at[0, 2], xr.at[0, 2], xp)
        arrived(upper, xr.at[1, 0])
        send(upper, upper, xs.at[1, 2], xr.at[1, 2], xm)

    def rest_weights():
        arrived(wf.at[wrow(nth(px, -1), 1)], xr.at[0, 1])
        arrived(wf.at[wrow(nth(px, 1), 0)], xr.at[1, 1])
        arrived(wf.at[wrow(nth(px, 2), 0)], xr.at[0, 2])
        arrived(wf.at[wrow(nth(px, 2), 1)], xr.at[1, 2])

    below, above = lax.rem(y + 3, 4), lax.rem(y + 1, 4)
    oc = 1 - core

    def forward_grads(fam):
        for k, (lo, hi) in enumerate(((olo, below // 2), (olo, above // 2), (ylo, 1 - yhi))):
            block = place(fam, lo, hi * 2 + core)
            arrived(block, yr.at[fam, k])
            send(block, block, cs.at[fam, k], cr.at[fam, k], pal)

    def rest_grads(fam):
        for k, (lo, hi) in enumerate(((olo, below // 2), (olo, above // 2), (ylo, 1 - yhi), (ylo, yhi))):
            arrived(place(fam, lo, hi * 2 + oc), cr.at[fam, k])

    def turn(slot, source, start, most):
        chunk = lax.min(start // 128, most)
        for i in range(3):
            lanes = pl.ds(pl.multiple_of((chunk + i) * 128, 128), 128)
            gt[slot, pl.ds(i * 128, 128), :] = source[:, lanes].T
        return pl.ds(pl.multiple_of(start - chunk * 128, 32), 224)

    def product(start, dst, extra=None):
        rows = turn(0, gf, start, (start // 896) * 7 + 4)

        def body(n, carry):
            cols = pl.ds(pl.multiple_of(n * 256, 256), 256)
            acc = jnp.dot(gt[0, rows, :], xf[:, cols], preferred_element_type=F32)
            if extra is not None:
                acc = acc + extra[:, cols].astype(F32)
            dst[:, cols] = acc.astype(dst.dtype)
            return carry
        lax.fori_loop(0, 4, body, 0)

    def signed_product(start, dst):
        rows = turn(0, sgf.at[pl.ds(0, 1280)], start, 4)
        turn(1, sgf.at[pl.ds(1280, 1280)], start, 4)

        def body(n, carry):
            cols = pl.ds(pl.multiple_of(n * 256, 256), 256)
            acc = jnp.dot(gt[0, rows, :], sxf[:, cols], preferred_element_type=F32)
            acc = acc + jnp.dot(gt[1, rows, :], sxp[:, cols], preferred_element_type=F32)
            dst[:, cols] = acc.astype(dst.dtype)
            return carry
        lax.fori_loop(0, 4, body, 0)

    def piece(k, h):
        return k * 448 + h * 224

    top, bot = pl.ds(0, 224), pl.ds(224, 224)

    def opposite():
        product(piece(nth(px, 2), 0), snd2.at[top])
        send(snd2.at[top], rhp, ps.at[0, 0], pr.at[0, 0], xp)
        product(piece(nth(px, 2), 1), snd2.at[bot])
        send(snd2.at[bot], rhm, ps.at[1, 0], pr.at[1, 0], xm)

    def beside():
        product(piece(nth(px, 1), 1), sndp.at[bot])
        send(sndp.at[bot], rom.at[bot], ps.at[0, 1], pr.at[0, 1], xp)
        product(piece(nth(px, -1), 0), sndm.at[top])
        send(sndm.at[top], rop.at[top], ps.at[1, 1], pr.at[1, 1], xm)

    def sideways():
        arrived(rhp, pr.at[0, 0])
        product(piece(nth(px, 1), 0), sndp.at[top], rhp)
        send(sndp.at[top], rom.at[top], ps.at[0, 2], pr.at[0, 2], xp)
        arrived(rhm, pr.at[1, 0])
        product(piece(nth(px, -1), 1), sndm.at[bot], rhm)
        send(sndm.at[bot], rop.at[bot], ps.at[1, 2], pr.at[1, 2], xm)

    def zfirst(u, buf, lo):
        send(buf.at[xrow(lo, nth(z, 2), 0)], rfp.at[u], ds.at[u, 0], dr.at[u, 0], zp)
        send(buf.at[xrow(lo, nth(z, 2), 1)], rfm.at[u], ds.at[u, 1], dr.at[u, 1], zm)
        send(buf.at[xrow(lo, nth(z, 1), 1)], rzm.at[u, pl.ds(80, 80)], ds.at[u, 2], dr.at[u, 2], zp)
        send(buf.at[xrow(lo, nth(z, -1), 0)], rzp.at[u, pl.ds(0, 80)], ds.at[u, 3], dr.at[u, 3], zm)

    def zsecond(u, buf, lo):
        rows = xrow(lo, nth(z, 1), 0)
        arrived(rfp.at[u], dr.at[u, 0])
        buf[rows, :] = (buf[rows, :].astype(F32) + rfp[u].astype(F32)).astype(BF16)
        send(buf.at[rows], rzm.at[u, pl.ds(0, 80)], ds.at[u, 4], dr.at[u, 4], zp)
        rows = xrow(lo, nth(z, -1), 1)
        arrived(rfm.at[u], dr.at[u, 1])
        buf[rows, :] = (buf[rows, :].astype(F32) + rfm[u].astype(F32)).astype(BF16)
        send(buf.at[rows], rzp.at[u, pl.ds(80, 80)], ds.at[u, 5], dr.at[u, 5], zm)

    def zsum(u, buf, lo):
        arrived(rzm.at[u, pl.ds(80, 80)], dr.at[u, 2])
        arrived(rzp.at[u, pl.ds(0, 80)], dr.at[u, 3])
        arrived(rzm.at[u, pl.ds(0, 80)], dr.at[u, 4])
        arrived(rzp.at[u, pl.ds(80, 80)], dr.at[u, 5])
        return buf[xblk(lo, z), :].astype(F32) + rzm[u].astype(F32) + rzp[u].astype(F32)

    def tokens(lo):
        return pl.ds(pl.multiple_of(lo * 640, 128), 640)

    def mate_part(u, lo):
        rows = tokens(lo)
        from_rows = pl.ds(pl.multiple_of(1280 + lo * 640, 128), 640)

        def body(n, carry):
            cols = pl.ds(pl.multiple_of(n * 256, 256), 256)
            dxp[rows, cols] = jnp.dot(sgf[from_rows, :], pf[:, cols], preferred_element_type=F32).astype(BF16)
            return carry
        lax.fori_loop(0, 4, body, 0)
        zfirst(u, dxp, lo)

    def own_part(u, lo):
        rows = tokens(lo)

        def body(n, carry):
            cols = pl.ds(pl.multiple_of(n * 256, 256), 256)
            a = jnp.dot(gf[rows, :], wf[:, cols], preferred_element_type=F32)
            b = jnp.dot(sgf[rows, :], pf[:, cols], preferred_element_type=F32)
            dxs[rows, cols] = (a + b * sf[rows, cols].astype(F32)).astype(BF16)
            return carry
        lax.fori_loop(0, 4, body, 0)
        zfirst(u, dxs, lo)

    forward_feats(0, ylo)
    for a in range(2):
        arrived(xdst[a].at[xblk(olo, z)], tr.at[a])
    send_feats(1, olo)

    @pl.loop(0, 5)
    def _(i):
        rows = pl.ds(pl.multiple_of((olo * 4 + z) * 160 + i * 32, 32), 32)
        sxf[rows, :] = xf[rows, :] * sf[rows, :]

    send(sxf.at[xblk(olo, z)], sxp.at[xblk(olo, z)], hs.at[1], hr.at[1], tmate)
    send_weights(1)
    forward_weights()
    arrived(parfar, gr.at[0])
    arrived(place(3, ylo, row), gr.at[1])
    send_grads(3)
    send_grads(2)
    forward_grads(0)
    forward_feats(1, olo)
    send_mates(0, ylo)
    forward_grads(1)
    send_mates(1, olo)
    rest_feats(0, ylo)
    rest_feats(1, olo)
    rest_grads(0)
    opposite()
    rest_grads(1)
    beside()
    forward_mates(0, ylo)
    forward_grads(3)
    for h in range(2):
        arrived(pf.at[wrow(1 - mine, h)], fr.at[h])
    forward_mates(1, olo)
    rest_grads(3)
    mate_part(0, olo)
    mate_part(1, ylo)
    for k in range(1, 4):
        for lo in (olo, ylo):
            @pl.loop(0, 5)
            def _(i, k=k, lo=lo):
                rows = pl.ds(pl.multiple_of((lo * 4 + nth(z, k)) * 160 + i * 32, 32), 32)
                sxf[rows, :] = xf[rows, :] * sf[rows, :]
    forward_grads(2)
    rest_grads(2)
    rest_weights()
    own_part(2, olo)
    sideways()
    zsecond(0, dxp, olo)
    rest_mates(0, ylo)
    rest_mates(1, olo)
    signed_product(piece(1 - mine, 0), ssnd.at[top])
    send(ssnd.at[top], srcv.at[top], qs.at[0], qr.at[0], fmate)
    own_part(3, ylo)
    zsecond(1, dxp, ylo)
    signed_product(piece(1 - mine, 1), ssnd.at[bot])
    send(ssnd.at[bot], srcv.at[bot], qs.at[1], qr.at[1], fmate)

    def to_mate(j, lo):
        tsnd[j] = zsum(j, dxp, lo).astype(BF16)
        send(tsnd.at[j], trcv.at[j], ks.at[j], kr.at[j], tmate)

    for h, part in enumerate((top, bot)):
        product(piece(px, h), mg.at[part])
    to_mate(0, olo)
    zsecond(2, dxs, olo)
    signed_product(piece(mine, 0), vg.at[top])
    to_mate(1, ylo)
    zsecond(3, dxs, ylo)
    signed_product(piece(mine, 1), vg.at[bot])

    def owned(j, lo):
        total = zsum(2 + j, dxs, lo)
        arrived(trcv.at[j], kr.at[j])
        return total + trcv[j].astype(F32) * sf[xblk(lo, z), :].astype(F32)

    ysnd[...] = owned(0, olo).astype(BF16)
    send(ysnd, yrcv, es.at[0], er.at[0], twin)

    def add(out, h, buf, last):
        def body(i, carry):
            rows = pl.ds(pl.multiple_of(h * 224 + i * 32, 32), 32)
            total = out[rows, :] + buf[rows, :].astype(F32)
            if last:
                total = total * scale
            if last == 2:
                total = total * nv[rows, :].astype(F32)
            out[rows, :] = total
            return carry
        lax.fori_loop(0, 7, body, 0)

    arrived(rom.at[bot], pr.at[0, 1])
    add(mg, 1, rom, 0)
    arrived(rop.at[top], pr.at[1, 1])
    add(mg, 0, rop, 0)
    arrived(rom.at[top], pr.at[0, 2])
    add(mg, 0, rom, 1)
    arrived(rop.at[bot], pr.at[1, 2])
    add(mg, 1, rop, 1)
    for h, part in enumerate((top, bot)):
        arrived(srcv.at[part], qr.at[h])
        add(vg, h, srcv, 2)
    final = owned(1, ylo)
    arrived(yrcv, er.at[0])
    ig[...] = (final + yrcv[...].astype(F32)).astype(BF16)
    for cp in sent:
        cp.wait_send()


def settle(a, b, c, oa, ob, oc, sem):
    moves = []
    for i, (src, dst) in enumerate(((b, ob), (c, oc), (a, oa))):
        n = src.shape[0] // 2
        for h in range(2):
            part = pl.ds(h * n, n)
            move = pltpu.make_async_copy(src.at[part], dst.at[part], sem.at[i, h])
            move.start()
            moves.append(move)
    for move in moves:
        move.wait()


def local(inputs, in_bits, out_grads, out_bits, mean_weight, sigma_weight, noise):
    count = inputs.shape[0] * lax.axis_size("depth") * lax.axis_size("col")
    hbm = pl.BlockSpec(memory_space=pltpu.HBM)
    vmem = pl.BlockSpec(memory_space=pltpu.VMEM)
    dma = pltpu.SemaphoreType.DMA
    V = pltpu.VMEM
    shapes = (jax.ShapeDtypeStruct((160, 1024), BF16), jax.ShapeDtypeStruct((448, 1024), F32),
              jax.ShapeDtypeStruct((448, 1024), F32))
    results = pl.pallas_call(
        functools.partial(kernel, count ** -0.5),
        out_shape=tuple(pltpu.VMEM(t.shape, t.dtype) for t in shapes),
        in_specs=[hbm] * 7,
        out_specs=(vmem,) * 3,
        scratch_shapes=[
            V((1792, 1024), BF16), V((896, 1024), BF16),
            V((1280, 1792), BF16), V((2560, 896), BF16),
            V((2, 384, 1280), BF16),
            V((1280, 1024), BF16), V((1280, 1024), BF16), V((1280, 1024), BF16), V((1280, 1024), BF16),
            V((160, 1792), BF16), V((160, 896), BF16), V((160, 896), BF16), V((160, 896), BF16),
            V((160, 896), BF16),
            V((160, 1024), jnp.int32), V((160, 1792), jnp.int32), V((160, 1792), jnp.int32),
            V((448, 1024), BF16),
            V((448, 1024), BF16), V((448, 1024), BF16), V((448, 1024), BF16),
            V((224, 1024), BF16), V((224, 1024), BF16),
            V((448, 1024), BF16), V((448, 1024), BF16),
            V((448, 1024), BF16), V((448, 1024), BF16),
            V((1280, 1024), BF16), V((1280, 1024), BF16),
            V((4, 80, 1024), BF16), V((4, 80, 1024), BF16), V((4, 160, 1024), BF16), V((4, 160, 1024), BF16),
            V((2, 160, 1024), BF16), V((2, 160, 1024), BF16),
            V((160, 1024), BF16), V((160, 1024), BF16),
            dma((9,)),
            dma((2, 3)), dma((2, 3)),
            dma((2, 2, 2, 3)), dma((2, 2, 2, 3)),
            dma((2, 2, 3)), dma((2, 2, 3)),
            dma((4, 3)), dma((4, 3)),
            dma((4, 4)), dma((4, 4)),
            dma((2,)), dma((2,)),
            dma((2,)), dma((2,)),
            dma((2,)), dma((2,)),
            dma((2,)), dma((2,)),
            dma((2, 3)), dma((2, 3)),
            dma((2,)), dma((2,)),
            dma((4, 6)), dma((4, 6)),
            dma((2,)), dma((2,)),
            dma((1,)), dma((1,)),
        ],
        compiler_params=pltpu.CompilerParams(collective_id=0, has_side_effects=True, vmem_limit_bytes=54 << 20),
        name="flipout_backward",
    )(*[pltpu.with_memory_space_constraint(t, pltpu.HBM) for t in (
        mean_weight, sigma_weight, noise, inputs, in_bits, out_grads, out_bits)])
    return pl.pallas_call(
        settle,
        out_shape=shapes,
        in_specs=[vmem] * 3,
        out_specs=(hbm, hbm, hbm),
        scratch_shapes=[dma((3, 2))],
        compiler_params=pltpu.CompilerParams(vmem_limit_bytes=8 << 20),
        name="settle",
    )(*results)


def solution(mesh):
    placed = (
        P(("depth", "col"), "row"),
        P(("depth", "col"), "row"),
        P(("depth", "row"), "col"),
        P(("depth", "row"), "col"),
        P(("col", "depth"), "row"),
        P(("col", "depth"), "row"),
        P(("col", "depth"), "row"),
    )
    return jax.shard_map(
        local,
        mesh=mesh,
        in_specs=placed,
        out_specs=(
            P(("depth", "col"), "row"),
            P(("col", "depth"), "row"),
            P(("col", "depth"), "row"),
        ),
        check_vma=False,
    )
```

```python
import functools
import jax
import jax.numpy as jnp
from jax import lax
from jax.experimental import pallas as pl
from jax.experimental.pallas import tpu as pltpu
from jax.sharding import PartitionSpec as P

F32 = jnp.float32
BF16 = jnp.bfloat16
MESH = pl.DeviceIdType.MESH
SPLIT = 512


def kernel(scale, w, sig, noise, x, ib, g, ob, ig, mg, vg,
           wf, pf, gf, sgf, gt, xf, sf, sxf, sxp, gfar, sgfar, sgno, sgfo, parfar, ibv, obn, obf, nv,
           snd2, sndp, sndm, rhp, rhm, rom, rop, ssnd, srcv, dxs, dxp, rfp, rfm, rzm, rzp,
           tsnd, trcv, ysnd, yrcv, ytw,
           lsem, xs, xr, zs, zr, us, ur, ys, yr, cs, cr, ts, tr, gs, gr, hs, hr, fs, fr,
           ps, pr, qs, qr, ds, dr, ks, kr, es, er):
    depth = lax.axis_index("depth")
    row = lax.axis_index("row")
    z = lax.axis_index("col")
    px = lax.rem(depth, 4)
    ylo = depth // 4
    core = lax.rem(row, 2)
    yhi = row // 2
    y = yhi * 2 + ylo
    olo = 1 - ylo
    mine = lax.rem(px, 2)
    pair = px // 2
    early = 1 - pair

    def dev(dx=0, dy=0, dz=0, dc=0):
        x2 = lax.rem(px + dx + 4, 4)
        y2 = lax.rem(y + dy + 4, 4)
        return (lax.rem(y2, 2) * 4 + x2, (y2 // 2) * 2 + lax.rem(core + dc, 2), lax.rem(z + dz + 4, 4))

    xp, xm = dev(1), dev(-1)
    zp, zm = dev(0, 0, 1), dev(0, 0, -1)
    yp, ym, y2 = dev(0, 1), dev(0, -1), dev(0, 2)
    pal = dev(0, 0, 0, 1)
    twin = (olo * 4 + px, row, z)
    fmate = (ylo * 4 + px + 1 - 2 * mine, row, z)
    tmate = (ylo * 4 + 3 - px, row, z)

    bar = pltpu.get_barrier_semaphore()
    for other in (xp, xm, zp, zm, yp, ym, y2, pal):
        pl.semaphore_signal(bar, inc=1, device_id=other, device_id_type=MESH)

    def here(src, dst, sem):
        cp = pltpu.make_async_copy(src, dst, sem)
        cp.start()
        return cp

    sent = []

    def send(src, dst, ssem, rsem, to):
        cp = pltpu.make_async_remote_copy(src_ref=src, dst_ref=dst, send_sem=ssem, recv_sem=rsem,
                                          device_id=to, device_id_type=MESH)
        cp.start()
        sent.append(cp)

    def arrived(dst, rsem):
        pltpu.make_async_remote_copy(src_ref=dst, dst_ref=dst, send_sem=rsem, recv_sem=rsem,
                                     device_id=pal, device_id_type=MESH).wait_recv()

    def wrow(k, h):
        return pl.ds(pl.multiple_of(k * 448 + h * 224, 32), 224)

    def xrow(lo, k, h):
        return pl.ds(pl.multiple_of((lo * 4 + k) * 160 + h * 80, 16), 80)

    def xblk(lo, k):
        return pl.ds(pl.multiple_of((lo * 4 + k) * 160, 32), 160)

    def half(lo):
        return pl.ds(pl.multiple_of(lo * 1792, 128), 1792)

    def quarter(q):
        return pl.ds(pl.multiple_of(q * 896, 128), 896)

    def nth(a, k):
        return lax.rem(a + k + 4, 4)

    def rows32(i):
        return pl.ds(pl.multiple_of(i * 32, 32), 32)

    xdst = (xf, sf)
    wown = pl.ds(pl.multiple_of(px * 448, 32), 448)
    xown = xblk(ylo, z)
    gown = xblk(ylo, row)
    load_w = here(w, wf.at[wown], lsem.at[0])
    load_x = here(x, xf.at[xown], lsem.at[1])
    load_ib = here(ib, ibv, lsem.at[2])
    load_gn = here(g.at[:, half(ylo)], gf.at[gown], lsem.at[3])
    load_gf = here(g.at[:, half(olo)], gfar, lsem.at[4])
    load_on = here(ob.at[:, half(ylo)], obn, lsem.at[5])
    load_of = here(ob.at[:, half(olo)], obf, lsem.at[6])
    load_s = here(sig, snd2, lsem.at[7])
    load_n = here(noise, nv, lsem.at[8])

    load_x.wait()
    load_ib.wait()

    @pl.loop(0, 5)
    def _(i):
        rows = pl.ds(pl.multiple_of((ylo * 4 + z) * 160 + i * 32, 32), 32)
        sign = (1 - 2 * ibv[rows32(i), :]).astype(BF16)
        sf[rows, :] = sign
        sxf[rows, :] = xf[rows, :] * sign

    load_w.wait()
    pl.semaphore_wait(bar, 8)

    def send_weights(h):
        send(wf.at[wrow(px, h)], wf.at[wrow(px, h)], xs.at[0, h], xr.at[0, h], xp)
        send(wf.at[wrow(px, 1 - h)], wf.at[wrow(px, 1 - h)], xs.at[1, h], xr.at[1, h], xm)

    def send_feats(part, lo):
        for h in range(2):
            for a in range(2):
                send(xdst[a].at[xrow(lo, z, h)], xdst[a].at[xrow(lo, z, h)],
                     zs.at[part, a, 0, h], zr.at[part, a, 0, h], zp)
                send(xdst[a].at[xrow(lo, z, 1 - h)], xdst[a].at[xrow(lo, z, 1 - h)],
                     zs.at[part, a, 1, h], zr.at[part, a, 1, h], zm)

    def place(fam, lo, r):
        if fam < 2:
            return gf.at[xblk(lo, r), quarter(early if fam == 0 else pair)]
        return sgf.at[pl.ds(pl.multiple_of((fam - 2) * 1280 + (lo * 4 + r) * 160, 32), 160)]

    def send_grads(fam):
        near = place(fam, ylo, row)
        if fam < 2:
            far = gfar.at[:, quarter(early if fam == 0 else pair)]
        else:
            far = sgfar if fam == 2 else parfar
        send(far, near, ys.at[fam, 0], yr.at[fam, 0], yp)
        send(far, near, ys.at[fam, 1], yr.at[fam, 1], ym)
        send(near, near, ys.at[fam, 2], yr.at[fam, 2], y2)
        send(near, near, cs.at[fam, 3], cr.at[fam, 3], pal)

    send_weights(0)
    for a in range(2):
        send(xdst[a].at[xown], xdst[a].at[xown], ts.at[a], tr.at[a], twin)
    send_feats(0, ylo)
    load_gn.wait()
    load_gf.wait()
    send_grads(0)
    load_on.wait()
    load_of.wait()

    @pl.loop(0, 5)
    def _(i):
        rows = rows32(i)
        own = pl.ds(pl.multiple_of((ylo * 4 + row) * 160 + i * 32, 32), 32)
        qa, qb = quarter(pair), quarter(early)
        sgf[own, :] = gf[own, qa] * (1 - 2 * obn[rows, qa]).astype(BF16)
        sgfar[rows, :] = gfar[rows, qa] * (1 - 2 * obf[rows, qa]).astype(BF16)
        sgno[rows, :] = gf[own, qb] * (1 - 2 * obn[rows, qb]).astype(BF16)
        sgfo[rows, :] = gfar[rows, qb] * (1 - 2 * obf[rows, qb]).astype(BF16)

    send(sgfo, parfar, gs.at[0], gr.at[0], tmate)
    send(sgno, place(3, ylo, row), gs.at[1], gr.at[1], tmate)
    send(sxf.at[xown], sxp.at[xown], hs.at[0], hr.at[0], tmate)
    load_s.wait()
    load_n.wait()

    @pl.loop(0, 14)
    def _(i):
        rows = rows32(i)
        own = pl.ds(pl.multiple_of(mine * 448 + i * 32, 32), 32)
        pf[own, :] = (snd2[rows, :].astype(F32) * nv[rows, :].astype(F32)).astype(BF16)

    for h in range(2):
        send(pf.at[wrow(mine, h)], pf.at[wrow(mine, h)], fs.at[h], fr.at[h], fmate)
    send_grads(1)

    def forward_feats(part, lo):
        for a in range(2):
            lower, upper = xdst[a].at[xrow(lo, nth(z, -1), 0)], xdst[a].at[xrow(lo, nth(z, 1), 1)]
            arrived(lower, zr.at[part, a, 0, 0])
            send(lower, lower, zs.at[part, a, 0, 2], zr.at[part, a, 0, 2], zp)
            arrived(upper, zr.at[part, a, 1, 0])
            send(upper, upper, zs.at[part, a, 1, 2], zr.at[part, a, 1, 2], zm)

    def rest_feats(part, lo):
        for a in range(2):
            arrived(xdst[a].at[xrow(lo, nth(z, -1), 1)], zr.at[part, a, 0, 1])
            arrived(xdst[a].at[xrow(lo, nth(z, 1), 0)], zr.at[part, a, 1, 1])
            arrived(xdst[a].at[xrow(lo, nth(z, 2), 0)], zr.at[part, a, 0, 2])
            arrived(xdst[a].at[xrow(lo, nth(z, 2), 1)], zr.at[part, a, 1, 2])

    def send_mates(part, lo):
        arrived(sxp.at[xblk(lo, z)], hr.at[part])
        for h in range(2):
            send(sxp.at[xrow(lo, z, h)], sxp.at[xrow(lo, z, h)], us.at[part, 0, h], ur.at[part, 0, h], zp)
            send(sxp.at[xrow(lo, z, 1 - h)], sxp.at[xrow(lo, z, 1 - h)], us.at[part, 1, h], ur.at[part, 1, h], zm)

    def forward_mates(part, lo):
        lower, upper = sxp.at[xrow(lo, nth(z, -1), 0)], sxp.at[xrow(lo, nth(z, 1), 1)]
        arrived(lower, ur.at[part, 0, 0])
        send(lower, lower, us.at[part, 0, 2], ur.at[part, 0, 2], zp)
        arrived(upper, ur.at[part, 1, 0])
        send(upper, upper, us.at[part, 1, 2], ur.at[part, 1, 2], zm)

    def rest_mates(part, lo):
        arrived(sxp.at[xrow(lo, nth(z, -1), 1)], ur.at[part, 0, 1])
        arrived(sxp.at[xrow(lo, nth(z, 1), 0)], ur.at[part, 1, 1])
        arrived(sxp.at[xrow(lo, nth(z, 2), 0)], ur.at[part, 0, 2])
        arrived(sxp.at[xrow(lo, nth(z, 2), 1)], ur.at[part, 1, 2])

    def forward_weights():
        lower, upper = wf.at[wrow(nth(px, -1), 0)], wf.at[wrow(nth(px, 1), 1)]
        arrived(lower, xr.at[0, 0])
        send(lower, lower, xs.at[0, 2], xr.at[0, 2], xp)
        arrived(upper, xr.at[1, 0])
        send(upper, upper, xs.at[1, 2], xr.at[1, 2], xm)

    def rest_weights():
        arrived(wf.at[wrow(nth(px, -1), 1)], xr.at[0, 1])
        arrived(wf.at[wrow(nth(px, 1), 0)], xr.at[1, 1])
        arrived(wf.at[wrow(nth(px, 2), 0)], xr.at[0, 2])
        arrived(wf.at[wrow(nth(px, 2), 1)], xr.at[1, 2])

    below, above = lax.rem(y + 3, 4), lax.rem(y + 1, 4)
    oc = 1 - core

    def forward_grads(fam):
        for k, (lo, hi) in enumerate(((olo, below // 2), (olo, above // 2), (ylo, 1 - yhi))):
            block = place(fam, lo, hi * 2 + core)
            arrived(block, yr.at[fam, k])
            send(block, block, cs.at[fam, k], cr.at[fam, k], pal)

    def rest_grads(fam):
        for k, (lo, hi) in enumerate(((olo, below // 2), (olo, above // 2), (ylo, 1 - yhi), (ylo, yhi))):
            arrived(place(fam, lo, hi * 2 + oc), cr.at[fam, k])

    def turn(slot, source, start, most):
        chunk = lax.min(start // 128, most)
        for i in range(3):
            lanes = pl.ds(pl.multiple_of((chunk + i) * 128, 128), 128)
            gt[slot, pl.ds(i * 128, 128), :] = source[:, lanes].T
        return pl.ds(pl.multiple_of(start - chunk * 128, 32), 224)

    def product(start, dst, extra=None):
        rows = turn(0, gf, start, (start // 896) * 7 + 4)

        def body(n, carry):
            cols = pl.ds(pl.multiple_of(n * 256, 256), 256)
            acc = jnp.dot(gt[0, rows, :], xf[:, cols], preferred_element_type=F32)
            if extra is not None:
                acc = acc + extra[:, cols].astype(F32)
            dst[:, cols] = acc.astype(dst.dtype)
            return carry
        lax.fori_loop(0, 4, body, 0)

    def signed_product(start, dst):
        rows = turn(0, sgf.at[pl.ds(0, 1280)], start, 4)
        turn(1, sgf.at[pl.ds(1280, 1280)], start, 4)

        def body(n, carry):
            cols = pl.ds(pl.multiple_of(n * 256, 256), 256)
            acc = jnp.dot(gt[0, rows, :], sxf[:, cols], preferred_element_type=F32)
            acc = acc + jnp.dot(gt[1, rows, :], sxp[:, cols], preferred_element_type=F32)
            dst[:, cols] = acc.astype(dst.dtype)
            return carry
        lax.fori_loop(0, 4, body, 0)

    def piece(k, h):
        return k * 448 + h * 224

    top, bot = pl.ds(0, 224), pl.ds(224, 224)

    def opposite():
        product(piece(nth(px, 2), 0), snd2.at[top])
        send(snd2.at[top], rhp, ps.at[0, 0], pr.at[0, 0], xp)
        product(piece(nth(px, 2), 1), snd2.at[bot])
        send(snd2.at[bot], rhm, ps.at[1, 0], pr.at[1, 0], xm)

    def beside():
        product(piece(nth(px, 1), 1), sndp.at[bot])
        send(sndp.at[bot], rom.at[bot], ps.at[0, 1], pr.at[0, 1], xp)
        product(piece(nth(px, -1), 0), sndm.at[top])
        send(sndm.at[top], rop.at[top], ps.at[1, 1], pr.at[1, 1], xm)

    def sideways():
        arrived(rhp, pr.at[0, 0])
        product(piece(nth(px, 1), 0), sndp.at[top], rhp)
        send(sndp.at[top], rom.at[top], ps.at[0, 2], pr.at[0, 2], xp)
        arrived(rhm, pr.at[1, 0])
        product(piece(nth(px, -1), 1), sndm.at[bot], rhm)
        send(sndm.at[bot], rop.at[bot], ps.at[1, 2], pr.at[1, 2], xm)

    def span(u):
        return pl.ds(0, SPLIT if u == 2 else 1024)

    def zfirst(u, buf, lo):
        c = span(u)
        send(buf.at[xrow(lo, nth(z, 2), 0), c], rfp.at[u, :, c], ds.at[u, 0], dr.at[u, 0], zp)
        send(buf.at[xrow(lo, nth(z, 2), 1), c], rfm.at[u, :, c], ds.at[u, 1], dr.at[u, 1], zm)
        send(buf.at[xrow(lo, nth(z, 1), 1), c], rzm.at[u, pl.ds(80, 80), c], ds.at[u, 2], dr.at[u, 2], zp)
        send(buf.at[xrow(lo, nth(z, -1), 0), c], rzp.at[u, pl.ds(0, 80), c], ds.at[u, 3], dr.at[u, 3], zm)

    def zsecond(u, buf, lo):
        c = span(u)
        rows = xrow(lo, nth(z, 1), 0)
        arrived(rfp.at[u, :, c], dr.at[u, 0])
        buf[rows, c] = (buf[rows, c].astype(F32) + rfp[u, :, c].astype(F32)).astype(BF16)
        send(buf.at[rows, c], rzm.at[u, pl.ds(0, 80), c], ds.at[u, 4], dr.at[u, 4], zp)
        rows = xrow(lo, nth(z, -1), 1)
        arrived(rfm.at[u, :, c], dr.at[u, 1])
        buf[rows, c] = (buf[rows, c].astype(F32) + rfm[u, :, c].astype(F32)).astype(BF16)
        send(buf.at[rows, c], rzp.at[u, pl.ds(80, 80), c], ds.at[u, 5], dr.at[u, 5], zm)

    def zsum(u, buf, lo):
        c = span(u)
        arrived(rzm.at[u, pl.ds(80, 80), c], dr.at[u, 2])
        arrived(rzp.at[u, pl.ds(0, 80), c], dr.at[u, 3])
        arrived(rzm.at[u, pl.ds(0, 80), c], dr.at[u, 4])
        arrived(rzp.at[u, pl.ds(80, 80), c], dr.at[u, 5])
        return buf[xblk(lo, z), c].astype(F32) + rzm[u, :, c].astype(F32) + rzp[u, :, c].astype(F32)

    def tokens(lo):
        return pl.ds(pl.multiple_of(lo * 640, 128), 640)

    def mate_part(u, lo):
        rows = tokens(lo)
        from_rows = pl.ds(pl.multiple_of(1280 + lo * 640, 128), 640)

        def body(n, carry):
            cols = pl.ds(pl.multiple_of(n * 256, 256), 256)
            dxp[rows, cols] = jnp.dot(sgf[from_rows, :], pf[:, cols], preferred_element_type=F32).astype(BF16)
            return carry
        lax.fori_loop(0, 4, body, 0)
        zfirst(u, dxp, lo)

    def own_part(lo, first, last):
        rows = tokens(lo)

        def body(n, carry):
            cols = pl.ds(pl.multiple_of(n * 256, 256), 256)
            a = jnp.dot(gf[rows, :], wf[:, cols], preferred_element_type=F32)
            b = jnp.dot(sgf[rows, :], pf[:, cols], preferred_element_type=F32)
            dxs[rows, cols] = (a + b * sf[rows, cols].astype(F32)).astype(BF16)
            return carry
        lax.fori_loop(first, last, body, 0)

    late = pl.ds(SPLIT, 1024 - SPLIT)

    forward_feats(0, ylo)
    for a in range(2):
        arrived(xdst[a].at[xblk(olo, z)], tr.at[a])
    send_feats(1, olo)

    @pl.loop(0, 5)
    def _(i):
        rows = pl.ds(pl.multiple_of((olo * 4 + z) * 160 + i * 32, 32), 32)
        sxf[rows, :] = xf[rows, :] * sf[rows, :]

    send(sxf.at[xblk(olo, z)], sxp.at[xblk(olo, z)], hs.at[1], hr.at[1], tmate)
    send_weights(1)
    forward_weights()
    arrived(parfar, gr.at[0])
    arrived(place(3, ylo, row), gr.at[1])
    send_grads(3)
    send_grads(2)
    forward_grads(0)
    forward_feats(1, olo)
    send_mates(0, ylo)
    forward_grads(1)
    send_mates(1, olo)
    rest_feats(0, ylo)
    rest_feats(1, olo)
    rest_grads(0)
    opposite()
    rest_grads(1)
    beside()
    forward_mates(0, ylo)
    forward_grads(3)
    for h in range(2):
        arrived(pf.at[wrow(1 - mine, h)], fr.at[h])
    forward_mates(1, olo)
    rest_grads(3)
    mate_part(0, olo)
    mate_part(1, ylo)
    for k in range(1, 4):
        for lo in (olo, ylo):
            @pl.loop(0, 5)
            def _(i, k=k, lo=lo):
                rows = pl.ds(pl.multiple_of((lo * 4 + nth(z, k)) * 160 + i * 32, 32), 32)
                sxf[rows, :] = xf[rows, :] * sf[rows, :]
    forward_grads(2)
    rest_grads(2)
    rest_weights()
    own_part(olo, SPLIT // 256, 4)
    send(dxs.at[tokens(olo), late], ytw, es.at[1], er.at[1], twin)
    own_part(olo, 0, SPLIT // 256)
    zfirst(2, dxs, olo)
    sideways()
    zsecond(0, dxp, olo)
    rest_mates(0, ylo)
    rest_mates(1, olo)
    signed_product(piece(1 - mine, 0), ssnd.at[top])
    send(ssnd.at[top], srcv.at[top], qs.at[0], qr.at[0], fmate)
    own_part(ylo, 0, 4)
    zsecond(1, dxp, ylo)
    signed_product(piece(1 - mine, 1), ssnd.at[bot])
    send(ssnd.at[bot], srcv.at[bot], qs.at[1], qr.at[1], fmate)
    arrived(ytw, er.at[1])

    @pl.loop(0, 20)
    def _(i):
        rows = pl.ds(pl.multiple_of(ylo * 640 + i * 32, 32), 32)
        dxs[rows, late] = (dxs[rows, late].astype(F32) + ytw[rows32(i), :].astype(F32)).astype(BF16)

    zfirst(3, dxs, ylo)

    def to_mate(j, lo):
        tsnd[j] = zsum(j, dxp, lo).astype(BF16)
        send(tsnd.at[j], trcv.at[j], ks.at[j], kr.at[j], tmate)

    for h, part in enumerate((top, bot)):
        product(piece(px, h), mg.at[part])
    to_mate(0, olo)
    zsecond(2, dxs, olo)
    signed_product(piece(mine, 0), vg.at[top])
    to_mate(1, ylo)
    zsecond(3, dxs, ylo)
    signed_product(piece(mine, 1), vg.at[bot])

    def owned(j, lo, c):
        return trcv[j, :, c].astype(F32) * sf[xblk(lo, z), c].astype(F32)

    first_sum = zsum(2, dxs, olo)
    arrived(trcv.at[0], kr.at[0])
    ysnd[:, span(2)] = (first_sum + owned(0, olo, span(2))).astype(BF16)
    ysnd[:, late] = owned(0, olo, late).astype(BF16)
    send(ysnd, yrcv, es.at[0], er.at[0], twin)

    def add(out, h, buf, last):
        def body(i, carry):
            rows = pl.ds(pl.multiple_of(h * 224 + i * 32, 32), 32)
            total = out[rows, :] + buf[rows, :].astype(F32)
            if last:
                total = total * scale
            if last == 2:
                total = total * nv[rows, :].astype(F32)
            out[rows, :] = total
            return carry
        lax.fori_loop(0, 7, body, 0)

    arrived(rom.at[bot], pr.at[0, 1])
    add(mg, 1, rom, 0)
    arrived(rop.at[top], pr.at[1, 1])
    add(mg, 0, rop, 0)
    arrived(rom.at[top], pr.at[0, 2])
    add(mg, 0, rom, 1)
    arrived(rop.at[bot], pr.at[1, 2])
    add(mg, 1, rop, 1)
    for h, part in enumerate((top, bot)):
        arrived(srcv.at[part], qr.at[h])
        add(vg, h, srcv, 2)
    final = zsum(3, dxs, ylo)
    arrived(trcv.at[1], kr.at[1])
    final = final + owned(1, ylo, span(3))
    arrived(yrcv, er.at[0])
    ig[...] = (final + yrcv[...].astype(F32)).astype(BF16)
    for cp in sent:
        cp.wait_send()


def settle(a, b, c, oa, ob, oc, sem):
    moves = []
    for i, (src, dst) in enumerate(((b, ob), (c, oc), (a, oa))):
        n = src.shape[0] // 2
        for h in range(2):
            part = pl.ds(h * n, n)
            move = pltpu.make_async_copy(src.at[part], dst.at[part], sem.at[i, h])
            move.start()
            moves.append(move)
    for move in moves:
        move.wait()


def local(inputs, in_bits, out_grads, out_bits, mean_weight, sigma_weight, noise):
    count = inputs.shape[0] * lax.axis_size("depth") * lax.axis_size("col")
    hbm = pl.BlockSpec(memory_space=pltpu.HBM)
    vmem = pl.BlockSpec(memory_space=pltpu.VMEM)
    dma = pltpu.SemaphoreType.DMA
    V = pltpu.VMEM
    shapes = (jax.ShapeDtypeStruct((160, 1024), BF16), jax.ShapeDtypeStruct((448, 1024), F32),
              jax.ShapeDtypeStruct((448, 1024), F32))
    results = pl.pallas_call(
        functools.partial(kernel, count ** -0.5),
        out_shape=tuple(pltpu.VMEM(t.shape, t.dtype) for t in shapes),
        in_specs=[hbm] * 7,
        out_specs=(vmem,) * 3,
        scratch_shapes=[
            V((1792, 1024), BF16), V((896, 1024), BF16),
            V((1280, 1792), BF16), V((2560, 896), BF16),
            V((2, 384, 1280), BF16),
            V((1280, 1024), BF16), V((1280, 1024), BF16), V((1280, 1024), BF16), V((1280, 1024), BF16),
            V((160, 1792), BF16), V((160, 896), BF16), V((160, 896), BF16), V((160, 896), BF16),
            V((160, 896), BF16),
            V((160, 1024), jnp.int32), V((160, 1792), jnp.int32), V((160, 1792), jnp.int32),
            V((448, 1024), BF16),
            V((448, 1024), BF16), V((448, 1024), BF16), V((448, 1024), BF16),
            V((224, 1024), BF16), V((224, 1024), BF16),
            V((448, 1024), BF16), V((448, 1024), BF16),
            V((448, 1024), BF16), V((448, 1024), BF16),
            V((1280, 1024), BF16), V((1280, 1024), BF16),
            V((4, 80, 1024), BF16), V((4, 80, 1024), BF16), V((4, 160, 1024), BF16), V((4, 160, 1024), BF16),
            V((2, 160, 1024), BF16), V((2, 160, 1024), BF16),
            V((160, 1024), BF16), V((160, 1024), BF16), V((640, 1024 - SPLIT), BF16),
            dma((9,)),
            dma((2, 3)), dma((2, 3)),
            dma((2, 2, 2, 3)), dma((2, 2, 2, 3)),
            dma((2, 2, 3)), dma((2, 2, 3)),
            dma((4, 3)), dma((4, 3)),
            dma((4, 4)), dma((4, 4)),
            dma((2,)), dma((2,)),
            dma((2,)), dma((2,)),
            dma((2,)), dma((2,)),
            dma((2,)), dma((2,)),
            dma((2, 3)), dma((2, 3)),
            dma((2,)), dma((2,)),
            dma((4, 6)), dma((4, 6)),
            dma((2,)), dma((2,)),
            dma((2,)), dma((2,)),
        ],
        compiler_params=pltpu.CompilerParams(collective_id=0, has_side_effects=True, vmem_limit_bytes=54 << 20),
        name="flipout_backward",
    )(*[pltpu.with_memory_space_constraint(t, pltpu.HBM) for t in (
        mean_weight, sigma_weight, noise, inputs, in_bits, out_grads, out_bits)])
    return pl.pallas_call(
        settle,
        out_shape=shapes,
        in_specs=[vmem] * 3,
        out_specs=(hbm, hbm, hbm),
        scratch_shapes=[dma((3, 2))],
        compiler_params=pltpu.CompilerParams(vmem_limit_bytes=8 << 20),
        name="settle",
    )(*results)


def solution(mesh):
    placed = (
        P(("depth", "col"), "row"),
        P(("depth", "col"), "row"),
        P(("depth", "row"), "col"),
        P(("depth", "row"), "col"),
        P(("col", "depth"), "row"),
        P(("col", "depth"), "row"),
        P(("col", "depth"), "row"),
    )
    return jax.shard_map(
        local,
        mesh=mesh,
        in_specs=placed,
        out_specs=(
            P(("depth", "col"), "row"),
            P(("col", "depth"), "row"),
            P(("col", "depth"), "row"),
        ),
        check_vma=False,
    )
```

```python
import functools
import jax
import jax.numpy as jnp
from jax import lax
from jax.experimental import pallas as pl
from jax.experimental.pallas import tpu as pltpu
from jax.sharding import PartitionSpec as P

F32 = jnp.float32
BF16 = jnp.bfloat16
MESH = pl.DeviceIdType.MESH
SPLIT = 512


def kernel(scale, w, sig, noise, x, ib, g, ob, ig, mg, vg,
           wf, pf, gf, sgf, gt, xf, sf, sxf, sxp, gfar, sgfar, sgno, sgfo, parfar, ibv, obn, obf, nv,
           snd2, sndp, sndm, rhp, rhm, rom, rop, ssnd, srcv, dxs, dxp, rfp, rfm, rzm, rzp,
           tsnd, trcv, ysnd, yrcv, ytw,
           lsem, xs, xr, zs, zr, us, ur, ys, yr, cs, cr, ts, tr, gs, gr, hs, hr, fs, fr,
           ps, pr, qs, qr, ds, dr, ks, kr, es, er):
    depth = lax.axis_index("depth")
    row = lax.axis_index("row")
    z = lax.axis_index("col")
    px = lax.rem(depth, 4)
    ylo = depth // 4
    core = lax.rem(row, 2)
    yhi = row // 2
    y = yhi * 2 + ylo
    olo = 1 - ylo
    mine = lax.rem(px, 2)
    pair = px // 2
    early = 1 - pair

    def dev(dx=0, dy=0, dz=0, dc=0):
        x2 = lax.rem(px + dx + 4, 4)
        y2 = lax.rem(y + dy + 4, 4)
        return (lax.rem(y2, 2) * 4 + x2, (y2 // 2) * 2 + lax.rem(core + dc, 2), lax.rem(z + dz + 4, 4))

    xp, xm = dev(1), dev(-1)
    zp, zm = dev(0, 0, 1), dev(0, 0, -1)
    yp, ym, y2 = dev(0, 1), dev(0, -1), dev(0, 2)
    pal = dev(0, 0, 0, 1)
    twin = (olo * 4 + px, row, z)
    fmate = (ylo * 4 + px + 1 - 2 * mine, row, z)
    tmate = (ylo * 4 + 3 - px, row, z)

    bar = pltpu.get_barrier_semaphore()
    for other in (xp, xm, zp, zm, yp, ym, y2, pal):
        pl.semaphore_signal(bar, inc=1, device_id=other, device_id_type=MESH)

    def here(src, dst, sem):
        cp = pltpu.make_async_copy(src, dst, sem)
        cp.start()
        return cp

    sent = []

    def send(src, dst, ssem, rsem, to):
        cp = pltpu.make_async_remote_copy(src_ref=src, dst_ref=dst, send_sem=ssem, recv_sem=rsem,
                                          device_id=to, device_id_type=MESH)
        cp.start()
        sent.append(cp)

    def arrived(dst, rsem):
        pltpu.make_async_remote_copy(src_ref=dst, dst_ref=dst, send_sem=rsem, recv_sem=rsem,
                                     device_id=pal, device_id_type=MESH).wait_recv()

    def wrow(k, h):
        return pl.ds(pl.multiple_of(k * 448 + h * 224, 32), 224)

    def xrow(lo, k, h):
        return pl.ds(pl.multiple_of((lo * 4 + k) * 160 + h * 80, 16), 80)

    def xblk(lo, k):
        return pl.ds(pl.multiple_of((lo * 4 + k) * 160, 32), 160)

    def half(lo):
        return pl.ds(pl.multiple_of(lo * 1792, 128), 1792)

    def quarter(q):
        return pl.ds(pl.multiple_of(q * 896, 128), 896)

    def nth(a, k):
        return lax.rem(a + k + 4, 4)

    def rows32(i):
        return pl.ds(pl.multiple_of(i * 32, 32), 32)

    xdst = (xf, sf)
    wown = pl.ds(pl.multiple_of(px * 448, 32), 448)
    xown = xblk(ylo, z)
    gown = xblk(ylo, row)
    load_w = here(w, wf.at[wown], lsem.at[0])
    load_x = here(x, xf.at[xown], lsem.at[1])
    load_ib = here(ib, ibv, lsem.at[2])
    load_gn = here(g.at[:, half(ylo)], gf.at[gown], lsem.at[3])
    load_gf = here(g.at[:, half(olo)], gfar, lsem.at[4])
    load_on = here(ob.at[:, half(ylo)], obn, lsem.at[5])
    load_of = here(ob.at[:, half(olo)], obf, lsem.at[6])
    load_s = here(sig, snd2, lsem.at[7])
    load_n = here(noise, nv, lsem.at[8])

    load_x.wait()
    load_ib.wait()

    @pl.loop(0, 5)
    def _(i):
        rows = pl.ds(pl.multiple_of((ylo * 4 + z) * 160 + i * 32, 32), 32)
        sign = (1 - 2 * ibv[rows32(i), :]).astype(BF16)
        sf[rows, :] = sign
        sxf[rows, :] = xf[rows, :] * sign

    load_w.wait()
    pl.semaphore_wait(bar, 8)

    def send_weights(h):
        send(wf.at[wrow(px, h)], wf.at[wrow(px, h)], xs.at[0, h], xr.at[0, h], xp)
        send(wf.at[wrow(px, 1 - h)], wf.at[wrow(px, 1 - h)], xs.at[1, h], xr.at[1, h], xm)

    def send_feats(part, lo):
        for h in range(2):
            for a in range(2):
                send(xdst[a].at[xrow(lo, z, h)], xdst[a].at[xrow(lo, z, h)],
                     zs.at[part, a, 0, h], zr.at[part, a, 0, h], zp)
                send(xdst[a].at[xrow(lo, z, 1 - h)], xdst[a].at[xrow(lo, z, 1 - h)],
                     zs.at[part, a, 1, h], zr.at[part, a, 1, h], zm)

    def place(fam, lo, r):
        if fam < 2:
            return gf.at[xblk(lo, r), quarter(early if fam == 0 else pair)]
        return sgf.at[pl.ds(pl.multiple_of((fam - 2) * 1280 + (lo * 4 + r) * 160, 32), 160)]

    def send_grads(fam):
        near = place(fam, ylo, row)
        if fam < 2:
            far = gfar.at[:, quarter(early if fam == 0 else pair)]
        else:
            far = sgfar if fam == 2 else parfar
        send(far, near, ys.at[fam, 0], yr.at[fam, 0], yp)
        send(far, near, ys.at[fam, 1], yr.at[fam, 1], ym)
        send(near, near, ys.at[fam, 2], yr.at[fam, 2], y2)
        send(near, near, cs.at[fam, 3], cr.at[fam, 3], pal)

    send_weights(0)
    for a in range(2):
        send(xdst[a].at[xown], xdst[a].at[xown], ts.at[a], tr.at[a], twin)
    send_feats(0, ylo)
    load_gn.wait()
    load_gf.wait()
    send_grads(0)
    load_on.wait()
    load_of.wait()

    @pl.loop(0, 5)
    def _(i):
        rows = rows32(i)
        own = pl.ds(pl.multiple_of((ylo * 4 + row) * 160 + i * 32, 32), 32)
        qa, qb = quarter(pair), quarter(early)
        sgf[own, :] = gf[own, qa] * (1 - 2 * obn[rows, qa]).astype(BF16)
        sgfar[rows, :] = gfar[rows, qa] * (1 - 2 * obf[rows, qa]).astype(BF16)
        sgno[rows, :] = gf[own, qb] * (1 - 2 * obn[rows, qb]).astype(BF16)
        sgfo[rows, :] = gfar[rows, qb] * (1 - 2 * obf[rows, qb]).astype(BF16)

    send(sgfo, parfar, gs.at[0], gr.at[0], tmate)
    send(sgno, place(3, ylo, row), gs.at[1], gr.at[1], tmate)
    send(sxf.at[xown], sxp.at[xown], hs.at[0], hr.at[0], tmate)
    load_s.wait()
    load_n.wait()

    @pl.loop(0, 14)
    def _(i):
        rows = rows32(i)
        own = pl.ds(pl.multiple_of(mine * 448 + i * 32, 32), 32)
        pf[own, :] = (snd2[rows, :].astype(F32) * nv[rows, :].astype(F32)).astype(BF16)

    for h in range(2):
        send(pf.at[wrow(mine, h)], pf.at[wrow(mine, h)], fs.at[h], fr.at[h], fmate)
    send_grads(1)

    def forward_feats(part, lo):
        for a in range(2):
            lower, upper = xdst[a].at[xrow(lo, nth(z, -1), 0)], xdst[a].at[xrow(lo, nth(z, 1), 1)]
            arrived(lower, zr.at[part, a, 0, 0])
            send(lower, lower, zs.at[part, a, 0, 2], zr.at[part, a, 0, 2], zp)
            arrived(upper, zr.at[part, a, 1, 0])
            send(upper, upper, zs.at[part, a, 1, 2], zr.at[part, a, 1, 2], zm)

    def rest_feats(part, lo):
        for a in range(2):
            arrived(xdst[a].at[xrow(lo, nth(z, -1), 1)], zr.at[part, a, 0, 1])
            arrived(xdst[a].at[xrow(lo, nth(z, 1), 0)], zr.at[part, a, 1, 1])
            arrived(xdst[a].at[xrow(lo, nth(z, 2), 0)], zr.at[part, a, 0, 2])
            arrived(xdst[a].at[xrow(lo, nth(z, 2), 1)], zr.at[part, a, 1, 2])

    def send_mates(part, lo):
        arrived(sxp.at[xblk(lo, z)], hr.at[part])
        for h in range(2):
            send(sxp.at[xrow(lo, z, h)], sxp.at[xrow(lo, z, h)], us.at[part, 0, h], ur.at[part, 0, h], zp)
            send(sxp.at[xrow(lo, z, 1 - h)], sxp.at[xrow(lo, z, 1 - h)], us.at[part, 1, h], ur.at[part, 1, h], zm)

    def forward_mates(part, lo):
        lower, upper = sxp.at[xrow(lo, nth(z, -1), 0)], sxp.at[xrow(lo, nth(z, 1), 1)]
        arrived(lower, ur.at[part, 0, 0])
        send(lower, lower, us.at[part, 0, 2], ur.at[part, 0, 2], zp)
        arrived(upper, ur.at[part, 1, 0])
        send(upper, upper, us.at[part, 1, 2], ur.at[part, 1, 2], zm)

    def rest_mates(part, lo):
        arrived(sxp.at[xrow(lo, nth(z, -1), 1)], ur.at[part, 0, 1])
        arrived(sxp.at[xrow(lo, nth(z, 1), 0)], ur.at[part, 1, 1])
        arrived(sxp.at[xrow(lo, nth(z, 2), 0)], ur.at[part, 0, 2])
        arrived(sxp.at[xrow(lo, nth(z, 2), 1)], ur.at[part, 1, 2])

    def forward_weights():
        lower, upper = wf.at[wrow(nth(px, -1), 0)], wf.at[wrow(nth(px, 1), 1)]
        arrived(lower, xr.at[0, 0])
        send(lower, lower, xs.at[0, 2], xr.at[0, 2], xp)
        arrived(upper, xr.at[1, 0])
        send(upper, upper, xs.at[1, 2], xr.at[1, 2], xm)

    def rest_weights():
        arrived(wf.at[wrow(nth(px, -1), 1)], xr.at[0, 1])
        arrived(wf.at[wrow(nth(px, 1), 0)], xr.at[1, 1])
        arrived(wf.at[wrow(nth(px, 2), 0)], xr.at[0, 2])
        arrived(wf.at[wrow(nth(px, 2), 1)], xr.at[1, 2])

    below, above = lax.rem(y + 3, 4), lax.rem(y + 1, 4)
    oc = 1 - core

    def forward_grads(fam):
        for k, (lo, hi) in enumerate(((olo, below // 2), (olo, above // 2), (ylo, 1 - yhi))):
            block = place(fam, lo, hi * 2 + core)
            arrived(block, yr.at[fam, k])
            send(block, block, cs.at[fam, k], cr.at[fam, k], pal)

    def rest_grads(fam):
        for k, (lo, hi) in enumerate(((olo, below // 2), (olo, above // 2), (ylo, 1 - yhi), (ylo, yhi))):
            arrived(place(fam, lo, hi * 2 + oc), cr.at[fam, k])

    def turn(slot, source, start, most):
        chunk = lax.min(start // 128, most)
        for i in range(3):
            lanes = pl.ds(pl.multiple_of((chunk + i) * 128, 128), 128)
            gt[slot, pl.ds(i * 128, 128), :] = source[:, lanes].T
        return pl.ds(pl.multiple_of(start - chunk * 128, 32), 224)

    def product(start, dst, extra=None):
        rows = turn(0, gf, start, (start // 896) * 7 + 4)

        def body(n, carry):
            cols = pl.ds(pl.multiple_of(n * 256, 256), 256)
            acc = jnp.dot(gt[0, rows, :], xf[:, cols], preferred_element_type=F32)
            if extra is not None:
                acc = acc + extra[:, cols].astype(F32)
            dst[:, cols] = acc.astype(dst.dtype)
            return carry
        lax.fori_loop(0, 4, body, 0)

    def signed_product(start, dst):
        rows = turn(0, sgf.at[pl.ds(0, 1280)], start, 4)
        turn(1, sgf.at[pl.ds(1280, 1280)], start, 4)

        def body(n, carry):
            cols = pl.ds(pl.multiple_of(n * 256, 256), 256)
            acc = jnp.dot(gt[0, rows, :], sxf[:, cols], preferred_element_type=F32)
            acc = acc + jnp.dot(gt[1, rows, :], sxp[:, cols], preferred_element_type=F32)
            dst[:, cols] = acc.astype(dst.dtype)
            return carry
        lax.fori_loop(0, 4, body, 0)

    def piece(k, h):
        return k * 448 + h * 224

    top, bot = pl.ds(0, 224), pl.ds(224, 224)

    def opposite():
        product(piece(nth(px, 2), 0), snd2.at[top])
        send(snd2.at[top], rhp, ps.at[0, 0], pr.at[0, 0], xp)
        product(piece(nth(px, 2), 1), snd2.at[bot])
        send(snd2.at[bot], rhm, ps.at[1, 0], pr.at[1, 0], xm)

    def beside():
        product(piece(nth(px, 1), 1), sndp.at[bot])
        send(sndp.at[bot], rom.at[bot], ps.at[0, 1], pr.at[0, 1], xp)
        product(piece(nth(px, -1), 0), sndm.at[top])
        send(sndm.at[top], rop.at[top], ps.at[1, 1], pr.at[1, 1], xm)

    def sideways():
        arrived(rhp, pr.at[0, 0])
        product(piece(nth(px, 1), 0), sndp.at[top], rhp)
        send(sndp.at[top], rom.at[top], ps.at[0, 2], pr.at[0, 2], xp)
        arrived(rhm, pr.at[1, 0])
        product(piece(nth(px, -1), 1), sndm.at[bot], rhm)
        send(sndm.at[bot], rop.at[bot], ps.at[1, 2], pr.at[1, 2], xm)

    def span(u):
        return pl.ds(0, SPLIT if u == 2 else 1024)

    def zfirst(u, buf, lo):
        c = span(u)
        send(buf.at[xrow(lo, nth(z, 2), 0), c], rfp.at[u, :, c], ds.at[u, 0], dr.at[u, 0], zp)
        send(buf.at[xrow(lo, nth(z, 2), 1), c], rfm.at[u, :, c], ds.at[u, 1], dr.at[u, 1], zm)
        send(buf.at[xrow(lo, nth(z, 1), 1), c], rzm.at[u, pl.ds(80, 80), c], ds.at[u, 2], dr.at[u, 2], zp)
        send(buf.at[xrow(lo, nth(z, -1), 0), c], rzp.at[u, pl.ds(0, 80), c], ds.at[u, 3], dr.at[u, 3], zm)

    def zsecond(u, buf, lo):
        c = span(u)
        rows = xrow(lo, nth(z, 1), 0)
        arrived(rfp.at[u, :, c], dr.at[u, 0])
        buf[rows, c] = (buf[rows, c].astype(F32) + rfp[u, :, c].astype(F32)).astype(BF16)
        send(buf.at[rows, c], rzm.at[u, pl.ds(0, 80), c], ds.at[u, 4], dr.at[u, 4], zp)
        rows = xrow(lo, nth(z, -1), 1)
        arrived(rfm.at[u, :, c], dr.at[u, 1])
        buf[rows, c] = (buf[rows, c].astype(F32) + rfm[u, :, c].astype(F32)).astype(BF16)
        send(buf.at[rows, c], rzp.at[u, pl.ds(80, 80), c], ds.at[u, 5], dr.at[u, 5], zm)

    def zsum(u, buf, lo):
        c = span(u)
        arrived(rzm.at[u, pl.ds(80, 80), c], dr.at[u, 2])
        arrived(rzp.at[u, pl.ds(0, 80), c], dr.at[u, 3])
        arrived(rzm.at[u, pl.ds(0, 80), c], dr.at[u, 4])
        arrived(rzp.at[u, pl.ds(80, 80), c], dr.at[u, 5])
        return buf[xblk(lo, z), c].astype(F32) + rzm[u, :, c].astype(F32) + rzp[u, :, c].astype(F32)

    def tokens(lo):
        return pl.ds(pl.multiple_of(lo * 640, 128), 640)

    def mate_part(u, lo):
        rows = tokens(lo)
        from_rows = pl.ds(pl.multiple_of(1280 + lo * 640, 128), 640)

        def body(n, carry):
            cols = pl.ds(pl.multiple_of(n * 256, 256), 256)
            dxp[rows, cols] = jnp.dot(sgf[from_rows, :], pf[:, cols], preferred_element_type=F32).astype(BF16)
            return carry
        lax.fori_loop(0, 4, body, 0)
        zfirst(u, dxp, lo)

    def own_part(lo, first, last):
        rows = tokens(lo)

        def body(n, carry):
            cols = pl.ds(pl.multiple_of(n * 256, 256), 256)
            a = jnp.dot(gf[rows, :], wf[:, cols], preferred_element_type=F32)
            b = jnp.dot(sgf[rows, :], pf[:, cols], preferred_element_type=F32)
            dxs[rows, cols] = (a + b * sf[rows, cols].astype(F32)).astype(BF16)
            return carry
        lax.fori_loop(first, last, body, 0)

    late = pl.ds(SPLIT, 1024 - SPLIT)

    forward_feats(0, ylo)
    for a in range(2):
        arrived(xdst[a].at[xblk(olo, z)], tr.at[a])
    send_feats(1, olo)

    @pl.loop(0, 5)
    def _(i):
        rows = pl.ds(pl.multiple_of((olo * 4 + z) * 160 + i * 32, 32), 32)
        sxf[rows, :] = xf[rows, :] * sf[rows, :]

    send(sxf.at[xblk(olo, z)], sxp.at[xblk(olo, z)], hs.at[1], hr.at[1], tmate)
    send_weights(1)
    forward_weights()
    arrived(parfar, gr.at[0])
    arrived(place(3, ylo, row), gr.at[1])
    send_grads(3)
    send_grads(2)
    forward_grads(0)
    forward_feats(1, olo)
    send_mates(0, ylo)
    forward_grads(1)
    send_mates(1, olo)
    rest_feats(0, ylo)
    rest_feats(1, olo)
    rest_grads(0)
    opposite()
    rest_grads(1)
    beside()
    forward_mates(0, ylo)
    forward_grads(3)
    for h in range(2):
        arrived(pf.at[wrow(1 - mine, h)], fr.at[h])
    forward_mates(1, olo)
    rest_grads(3)
    mate_part(0, olo)
    mate_part(1, ylo)
    for k in range(1, 4):
        for lo in (olo, ylo):
            @pl.loop(0, 5)
            def _(i, k=k, lo=lo):
                rows = pl.ds(pl.multiple_of((lo * 4 + nth(z, k)) * 160 + i * 32, 32), 32)
                sxf[rows, :] = xf[rows, :] * sf[rows, :]
    forward_grads(2)
    rest_grads(2)
    rest_weights()
    own_part(olo, SPLIT // 256, 4)
    send(dxs.at[tokens(olo), late], ytw, es.at[1], er.at[1], twin)
    own_part(olo, 0, SPLIT // 256)
    zfirst(2, dxs, olo)
    sideways()
    zsecond(0, dxp, olo)
    rest_mates(0, ylo)
    rest_mates(1, olo)
    signed_product(piece(1 - mine, 0), ssnd.at[top])
    send(ssnd.at[top], srcv.at[top], qs.at[0], qr.at[0], fmate)
    def to_mate(j, lo):
        tsnd[j] = zsum(j, dxp, lo).astype(BF16)
        send(tsnd.at[j], trcv.at[j], ks.at[j], kr.at[j], tmate)

    def owned(j, lo, c):
        return trcv[j, :, c].astype(F32) * sf[xblk(lo, z), c].astype(F32)

    zsecond(1, dxp, ylo)
    signed_product(piece(1 - mine, 1), ssnd.at[bot])
    send(ssnd.at[bot], srcv.at[bot], qs.at[1], qr.at[1], fmate)
    own_part(ylo, 0, 4)
    arrived(ytw, er.at[1])

    @pl.loop(0, 20)
    def _(i):
        rows = pl.ds(pl.multiple_of(ylo * 640 + i * 32, 32), 32)
        dxs[rows, late] = (dxs[rows, late].astype(F32) + ytw[rows32(i), :].astype(F32)).astype(BF16)

    zfirst(3, dxs, ylo)
    zsecond(2, dxs, olo)
    to_mate(0, olo)
    to_mate(1, ylo)
    for h, part in enumerate((top, bot)):
        product(piece(px, h), mg.at[part])
    zsecond(3, dxs, ylo)
    first_sum = zsum(2, dxs, olo)
    arrived(trcv.at[0], kr.at[0])
    ysnd[:, span(2)] = (first_sum + owned(0, olo, span(2))).astype(BF16)
    ysnd[:, late] = owned(0, olo, late).astype(BF16)
    send(ysnd, yrcv, es.at[0], er.at[0], twin)
    signed_product(piece(mine, 0), vg.at[top])
    signed_product(piece(mine, 1), vg.at[bot])

    def add(out, h, buf, last):
        def body(i, carry):
            rows = pl.ds(pl.multiple_of(h * 224 + i * 32, 32), 32)
            total = out[rows, :] + buf[rows, :].astype(F32)
            if last:
                total = total * scale
            if last == 2:
                total = total * nv[rows, :].astype(F32)
            out[rows, :] = total
            return carry
        lax.fori_loop(0, 7, body, 0)

    arrived(rom.at[bot], pr.at[0, 1])
    add(mg, 1, rom, 0)
    arrived(rop.at[top], pr.at[1, 1])
    add(mg, 0, rop, 0)
    arrived(rom.at[top], pr.at[0, 2])
    add(mg, 0, rom, 1)
    arrived(rop.at[bot], pr.at[1, 2])
    add(mg, 1, rop, 1)
    for h, part in enumerate((top, bot)):
        arrived(srcv.at[part], qr.at[h])
        add(vg, h, srcv, 2)
    final = zsum(3, dxs, ylo)
    arrived(trcv.at[1], kr.at[1])
    final = final + owned(1, ylo, span(3))
    arrived(yrcv, er.at[0])
    ig[...] = (final + yrcv[...].astype(F32)).astype(BF16)
    for cp in sent:
        cp.wait_send()


def settle(a, b, c, oa, ob, oc, sem):
    moves = []
    for i, (src, dst) in enumerate(((b, ob), (c, oc), (a, oa))):
        n = src.shape[0] // 2
        for h in range(2):
            part = pl.ds(h * n, n)
            move = pltpu.make_async_copy(src.at[part], dst.at[part], sem.at[i, h])
            move.start()
            moves.append(move)
    for move in moves:
        move.wait()


def local(inputs, in_bits, out_grads, out_bits, mean_weight, sigma_weight, noise):
    count = inputs.shape[0] * lax.axis_size("depth") * lax.axis_size("col")
    hbm = pl.BlockSpec(memory_space=pltpu.HBM)
    vmem = pl.BlockSpec(memory_space=pltpu.VMEM)
    dma = pltpu.SemaphoreType.DMA
    V = pltpu.VMEM
    shapes = (jax.ShapeDtypeStruct((160, 1024), BF16), jax.ShapeDtypeStruct((448, 1024), F32),
              jax.ShapeDtypeStruct((448, 1024), F32))
    results = pl.pallas_call(
        functools.partial(kernel, count ** -0.5),
        out_shape=tuple(pltpu.VMEM(t.shape, t.dtype) for t in shapes),
        in_specs=[hbm] * 7,
        out_specs=(vmem,) * 3,
        scratch_shapes=[
            V((1792, 1024), BF16), V((896, 1024), BF16),
            V((1280, 1792), BF16), V((2560, 896), BF16),
            V((2, 384, 1280), BF16),
            V((1280, 1024), BF16), V((1280, 1024), BF16), V((1280, 1024), BF16), V((1280, 1024), BF16),
            V((160, 1792), BF16), V((160, 896), BF16), V((160, 896), BF16), V((160, 896), BF16),
            V((160, 896), BF16),
            V((160, 1024), jnp.int32), V((160, 1792), jnp.int32), V((160, 1792), jnp.int32),
            V((448, 1024), BF16),
            V((448, 1024), BF16), V((448, 1024), BF16), V((448, 1024), BF16),
            V((224, 1024), BF16), V((224, 1024), BF16),
            V((448, 1024), BF16), V((448, 1024), BF16),
            V((448, 1024), BF16), V((448, 1024), BF16),
            V((1280, 1024), BF16), V((1280, 1024), BF16),
            V((4, 80, 1024), BF16), V((4, 80, 1024), BF16), V((4, 160, 1024), BF16), V((4, 160, 1024), BF16),
            V((2, 160, 1024), BF16), V((2, 160, 1024), BF16),
            V((160, 1024), BF16), V((160, 1024), BF16), V((640, 1024 - SPLIT), BF16),
            dma((9,)),
            dma((2, 3)), dma((2, 3)),
            dma((2, 2, 2, 3)), dma((2, 2, 2, 3)),
            dma((2, 2, 3)), dma((2, 2, 3)),
            dma((4, 3)), dma((4, 3)),
            dma((4, 4)), dma((4, 4)),
            dma((2,)), dma((2,)),
            dma((2,)), dma((2,)),
            dma((2,)), dma((2,)),
            dma((2,)), dma((2,)),
            dma((2, 3)), dma((2, 3)),
            dma((2,)), dma((2,)),
            dma((4, 6)), dma((4, 6)),
            dma((2,)), dma((2,)),
            dma((2,)), dma((2,)),
        ],
        compiler_params=pltpu.CompilerParams(collective_id=0, has_side_effects=True, vmem_limit_bytes=54 << 20),
        name="flipout_backward",
    )(*[pltpu.with_memory_space_constraint(t, pltpu.HBM) for t in (
        mean_weight, sigma_weight, noise, inputs, in_bits, out_grads, out_bits)])
    return pl.pallas_call(
        settle,
        out_shape=shapes,
        in_specs=[vmem] * 3,
        out_specs=(hbm, hbm, hbm),
        scratch_shapes=[dma((3, 2))],
        compiler_params=pltpu.CompilerParams(vmem_limit_bytes=8 << 20),
        name="settle",
    )(*results)


def solution(mesh):
    placed = (
        P(("depth", "col"), "row"),
        P(("depth", "col"), "row"),
        P(("depth", "row"), "col"),
        P(("depth", "row"), "col"),
        P(("col", "depth"), "row"),
        P(("col", "depth"), "row"),
        P(("col", "depth"), "row"),
    )
    return jax.shard_map(
        local,
        mesh=mesh,
        in_specs=placed,
        out_specs=(
            P(("depth", "col"), "row"),
            P(("col", "depth"), "row"),
            P(("col", "depth"), "row"),
        ),
        check_vma=False,
    )
```
